256 devices in a mesh: dp: 4 (over x), expert: 64 (over z, y, core).
Axes of the slice: x: 4, y: 4, z: 8, core: 2. Of those that a mesh axis runs over, the one named last changes fastest.
Arguments:
- tokens: bfloat16 [32768, 7168], P(('dp', 'expert')), may hold values from -6 to 6
- cotangent: bfloat16 [32768, 7168], P(('dp', 'expert')), may hold values from -6 to 6
- route_ids: int32 [32768, 8], P(('dp', 'expert')), may hold values from 0 to 255, all different within a row; in each aligned block of 128 rows (0 to 127, 128 to 255, ...) at most 5 rows name the same one
- router_weights: float32 [32768, 8], P(('dp', 'expert')), may hold values from 0.05 to 0.3
- master: float32 [64, 7168, 384], P('expert', 'dp'), may hold values from -0.0625 to 0.0625
- accumulator: float32 [64, 3, 7168], P('expert', None, 'dp'), may hold values from 0.1 to 10
Outputs:
- output: bfloat16 [32768, 7168], P(('dp', 'expert'))
- input_grad: bfloat16 [32768, 7168], P(('dp', 'expert'))
- new_weights: bfloat16 [64, 7168, 384], P('expert', 'dp')
- accumulator_out: float32 [64, 3, 7168], P('expert', None, 'dp')
The draws below stay inside these ranges and needn't reach their ends.
Inputs may be any that keep to these rules, and one draw needn't show every extreme that they name: `route_ids`: each row names distinct experts. In each aligned block of 128 rows (the rows of one device) no expert is named by more than 5 rows, a bound that some block reaches.
All inputs are finite; a program needn't handle non-finite values.
Results may differ from the reference program's by a relative error of at most 0.011.
Values may be sent and summed in bfloat16 or wider, within the bound.
No kernel may reach another device: no remote copies, remote signals or barrier semaphores. Data moves between devices by JAX's collectives and lax.ppermute only.
A program may use at most 128 MiB of HBM per device.

```python
import math
import jax
import jax.numpy as jnp
import numpy as np
from jax import lax

D = 7168
SLICES = 8
TOP = 8
TOK_DEV = 128
H_DEV = 128
EXPERTS = 256
GROUP = 8
SLOTS = 64
CAP = 5
TOKENS = 32768
N_DP = 4
N_EXPERT = 64


def level_of(key, dims, shards, least, high):
    def one(axis_at, shards_of):
        steps = jax.random.uniform(jax.random.fold_in(jax.random.fold_in(key, 6), axis_at), (shards_of,), jnp.float32, least / len(shards), high / len(shards))
        return jnp.repeat(jnp.exp(steps), dims[axis_at] // shards_of).reshape((-1,) + (1,) * (len(dims) - axis_at - 1))

    level = one(*shards[0])
    for cut in shards[1:]:
        level = level * one(*cut)
    return level


def assign_block(key, own, number, rows, count, top, limit, lean):
    order = jax.random.permutation(key, count)
    packed, common = shares(count, rows * top, limit, lean, True), shares(count, rows * top, limit, lean, False)
    places = jnp.arange(count)

    def named(lengths, offset_by):
        used = int((lengths > 0).sum())
        fixed = max(1, used // 4)
        shifted = fixed + (places - fixed + offset_by * (used - fixed)) % max(1, count - fixed)
        return jnp.zeros((count,), jnp.int32).at[order[jnp.where(places < fixed, places, shifted)]].set(jnp.asarray(lengths, jnp.int32))

    lengths = jnp.where(number % 4 == 0, named(packed, number // 4), named(common, number - number // 4 - 1))
    mixed = jax.random.permutation(jax.random.fold_in(own, 3), count)
    giver, taker = mixed[0:count // 2 * 2:2], mixed[1:count // 2 * 2:2]
    margin = jnp.minimum(lengths[giver] - 1, limit - lengths[taker]) // 2
    margin = jnp.where((giver == order[0]) | (taker == order[0]) | (lengths[taker] == 0), 0, jnp.maximum(margin, 0))
    shifted = jax.random.randint(jax.random.fold_in(own, 4), (count // 2,), 0, 1 << 20) % (margin + 1)
    lengths = lengths.at[giver].add(-shifted).at[taker].add(shifted)
    items = jnp.searchsorted(jnp.cumsum(lengths), jnp.arange(rows * top), side="right").astype(jnp.int32)
    table = items.reshape(top, rows).T
    table = table[jax.random.permutation(jax.random.fold_in(own, 1), rows)]
    offset_by = jax.random.randint(jax.random.fold_in(own, 2), (rows, 1), 0, top)
    return jnp.take_along_axis(table, (jnp.arange(top)[None, :] + offset_by) % top, axis=1)


def shares(number_of, total, bound, lean, full):
    portions = [(1 << 20) // math.isqrt(rank ** lean) + 1 for rank in range(1, number_of + 1)]
    largest = bound if full else min(bound, max(-(-total // number_of), total * portions[0] // sum(portions)))
    least = 1 if total - largest >= number_of - 1 else 0
    counts, rest = [largest] + [least] * (number_of - 1), total - largest - least * (number_of - 1)
    while rest > 0:
        candidates = [i for i in range(1, number_of) if counts[i] < largest] or [i for i in range(1, number_of) if counts[i] < bound]
        pool, remaining = sum([portions[i] for i in candidates]), rest
        for i in candidates:
            addition = min(bound - counts[i], max(1, remaining * portions[i] // pool), rest)
            counts[i] = counts[i] + addition
            rest = rest - addition
    return np.array(counts)


def bell_draw(stream_key, dims, deviation, bound, split=(), kind=jnp.bfloat16):
    entries = deviation * jax.random.normal(stream_key, dims, jnp.float32)
    if split:
        entries = entries * level_of(stream_key, dims, split, -0.22, 0.18)
    return jnp.clip(entries, -bound, bound).astype(kind)


def setup_inputs(seed: int = 0) -> dict:
    key_of = jax.random.split(jax.random.key(seed), 7)
    tokens = bell_draw(key_of[0], (TOKENS, D), 1.0, 6.0, ((0, 256),))
    cotangent = bell_draw(key_of[1], (TOKENS, D), 1.0, 6.0, ((0, 256),))
    route_ids_keys = jax.random.split(jax.random.fold_in(key_of[2], 1), TOKENS // TOK_DEV)
    route_ids_turns = jax.random.permutation(jax.random.fold_in(key_of[2], 3), TOKENS // TOK_DEV)
    route_ids = jax.vmap(lambda own, number: assign_block(jax.random.fold_in(key_of[2], 2), own, number, TOK_DEV, EXPERTS, TOP, CAP, 2))(route_ids_keys, route_ids_turns).reshape((TOKENS, TOP))
    router_weights = jnp.clip(0.05 + 0.25 * jax.random.uniform(key_of[3], (TOKENS, TOP), jnp.float32) ** level_of(key_of[3], (TOKENS, TOP), ((0, 256),), -0.2, 0.2), 0.05, 0.3)
    master = bell_draw(key_of[4], (SLOTS, D, 3 * H_DEV), D ** -0.5, 0.0625, ((0, 64), (1, 4)), jnp.float32)
    accumulator = jnp.clip(jnp.exp(math.log(10.0) - 4.6051702 * jax.random.uniform(key_of[5], (SLOTS, 3, D), jnp.float32) ** level_of(key_of[5], (SLOTS, 3, D), ((0, 64), (2, 4)), -0.2, 0.2)), 0.1, 10.0)
    return dict(tokens=tokens, cotangent=cotangent, route_ids=route_ids, router_weights=router_weights, master=master, accumulator=accumulator)


LEARN_RATE = 0.01
EPSILON = 1e-06

def slot_table(block_ids, live_count, capacity):
    flat_ids = block_ids.reshape(-1)
    onehot = (flat_ids[:, None] == jnp.arange(live_count, dtype=jnp.int32)[None, :]).astype(jnp.int32)
    before = jnp.cumsum(onehot, axis=0) - onehot
    position = lax.optimization_barrier(jnp.sum(before * onehot, axis=1))
    return jnp.where(flat_ids < live_count, flat_ids * capacity + position, live_count * capacity).astype(jnp.int32)

def pair_flip(array):
    shape = array.shape
    return array.reshape((shape[0] // 2, 2) + shape[1:])[:, ::-1].reshape(shape)

def expert_pass(operands):
    in_rows, cot_rows, slice_weights = operands
    hdev = H_DEV
    x_full = in_rows.astype(jnp.float32)
    d_full = cot_rows.astype(jnp.float32)
    w_full = slice_weights.astype(jnp.float32)
    high = lax.Precision.HIGHEST
    gate_up = jnp.einsum('rd,sdh->srh', x_full, w_full[:, :, :2 * hdev], precision=high)
    gate_pre = gate_up[:, :, :hdev]
    up_pre = gate_up[:, :, hdev:]
    sigmoid_gate = jax.nn.sigmoid(gate_pre)
    silu_gate = gate_pre * sigmoid_gate
    hidden = (silu_gate * up_pre).astype(jnp.bfloat16)
    hidden_full = hidden.astype(jnp.float32)
    down_cols = w_full[:, :, 2 * hdev:]
    out_part = jnp.einsum('srh,sdh->srd', hidden_full, down_cols, precision=high).astype(jnp.bfloat16)
    grad_hidden = jnp.einsum('rd,sdh->srh', d_full, down_cols, precision=high)
    grad_gate = grad_hidden * up_pre * sigmoid_gate * (1.0 + gate_pre * (1.0 - sigmoid_gate))
    grad_up = grad_hidden * silu_gate
    grad_pre = jnp.concatenate([grad_gate, grad_up], axis=2).astype(jnp.bfloat16)
    grad_full = grad_pre.astype(jnp.float32)
    in_part = jnp.einsum('srk,sdk->srd', grad_full, w_full[:, :, :2 * hdev], precision=high).astype(jnp.bfloat16)
    grad_in = jnp.einsum('rd,srk->sdk', x_full, grad_full, precision=high)
    grad_down = jnp.einsum('rd,srh->sdh', d_full, hidden_full, precision=high)
    replica_grad = jnp.concatenate([grad_in, grad_down], axis=2).astype(jnp.bfloat16)
    return (out_part, in_part, replica_grad)

def reference(tokens, cotangent, route_ids, router_weights, master, accumulator):
    devices_e = N_EXPERT
    tok_rows = TOK_DEV
    live_count = GROUP
    capacity = CAP
    hdev = H_DEV
    width = live_count * capacity
    working = pair_flip(master).astype(jnp.bfloat16).reshape(live_count, SLICES, D, 3 * hdev)
    total = jnp.zeros((SLOTS, D, 3 * hdev), jnp.float32)
    outputs = []
    in_grads = []
    device_rows = jnp.arange(devices_e, dtype=jnp.int32)[:, None]
    token_of = jnp.repeat(jnp.arange(tok_rows, dtype=jnp.int32), TOP)
    for replica in range(N_DP):
        start = replica * devices_e * tok_rows
        stop = start + devices_e * tok_rows
        x_rep = tokens[start:stop].reshape(devices_e, tok_rows, D)
        c_rep = cotangent[start:stop].reshape(devices_e, tok_rows, D)
        ids_rep = route_ids[start:stop].reshape(devices_e, tok_rows, TOP)
        w_rep = router_weights[start:stop].reshape(devices_e, tok_rows * TOP)
        slot_ids = jax.vmap(lambda block: slot_table(block, live_count, capacity))(ids_rep)
        source = jnp.broadcast_to(token_of[None, :], slot_ids.shape)
        index = jnp.zeros((devices_e, width), jnp.int32).at[device_rows, slot_ids].set(source, mode='drop')
        filled = jnp.zeros((devices_e, width), jnp.float32).at[device_rows, slot_ids].set(1.0, mode='drop')
        weight_slot = jnp.zeros((devices_e, width), jnp.float32).at[device_rows, slot_ids].set(w_rep, mode='drop')
        x_sel = jax.vmap(lambda rows, picks: rows[picks])(x_rep, index)
        c_sel = jax.vmap(lambda rows, picks: rows[picks])(c_rep, index)
        x_sel = jnp.where(filled[:, :, None] > 0, x_sel, jnp.zeros_like(x_sel))
        d_sel = (c_sel.astype(jnp.float32) * weight_slot[:, :, None]).astype(jnp.bfloat16)
        x_exp = x_sel.reshape(devices_e, live_count, capacity, D).transpose(1, 0, 2, 3).reshape(live_count, devices_e * capacity, D)
        d_exp = d_sel.reshape(devices_e, live_count, capacity, D).transpose(1, 0, 2, 3).reshape(live_count, devices_e * capacity, D)
        out_part, in_part, replica_grad = lax.map(expert_pass, (x_exp, d_exp, working))
        out_sum = lax.optimization_barrier(jnp.sum(out_part.astype(jnp.float32), axis=1))
        in_sum = lax.optimization_barrier(jnp.sum(in_part.astype(jnp.float32), axis=1))
        out_sum = out_sum.reshape(live_count, devices_e, capacity, D).transpose(1, 0, 2, 3).reshape(devices_e, width, D)
        in_sum = in_sum.reshape(live_count, devices_e, capacity, D).transpose(1, 0, 2, 3).reshape(devices_e, width, D)
        y_rep = jnp.zeros((devices_e, tok_rows, D), jnp.float32).at[device_rows, index].add(out_sum * weight_slot[:, :, None])
        dx_rep = jnp.zeros((devices_e, tok_rows, D), jnp.float32).at[device_rows, index].add(in_sum * filled[:, :, None])
        outputs.append(y_rep.reshape(devices_e * tok_rows, D).astype(jnp.bfloat16))
        in_grads.append(dx_rep.reshape(devices_e * tok_rows, D).astype(jnp.bfloat16))
        total = total + replica_grad.reshape(SLOTS, D, 3 * hdev).astype(jnp.float32)
    gradient = total.astype(jnp.bfloat16)
    grad_master = pair_flip(gradient).astype(jnp.float32).reshape(SLOTS, D, 3, hdev)
    mean_square = lax.optimization_barrier(jnp.mean(grad_master * grad_master, axis=3))
    accumulator_out = accumulator + mean_square.transpose(0, 2, 1)
    scale = 1.0 / (jnp.sqrt(accumulator_out) + EPSILON)
    update = grad_master * scale.transpose(0, 2, 1)[:, :, :, None]
    master_new = master - LEARN_RATE * update.reshape(SLOTS, D, 3 * hdev)
    new_weights = pair_flip(master_new).astype(jnp.bfloat16)
    output = jnp.concatenate(outputs, axis=0)
    input_grad = jnp.concatenate(in_grads, axis=0)
    return (output, input_grad, new_weights, accumulator_out)
```

```python
import functools

import jax
import jax.numpy as jnp
from jax import lax
from jax.experimental import pallas as pl
from jax.experimental.pallas import tpu as pltpu
from jax.sharding import Mesh, PartitionSpec as P


N_X, N_Z, N_Y, N_C = 4, 8, 4, 2
CAP = 5
LEARN_RATE = 0.01
EPSILON = 1e-06
BF = jnp.bfloat16
F32 = jnp.float32
ROWS = 2 * CAP
PACK = N_X * ROWS


def swap_core(a):
    return lax.ppermute(a, "c", [(0, 1), (1, 0)])


def iota(shape, dim):
    return lax.broadcasted_iota(jnp.int32, shape, dim)


def select_kernel(ids_ref, w_ref, tok_ref, cot_ref, send_ref, tab_ref, sel_ref, row_ref, acc_ref):
    q = pl.program_id(1)
    first = (pl.program_id(0) == 0) & (q == 0)

    @pl.when(first)
    def _():
        rows = ids_ref.shape[0]
        lane = iota((rows, 128), 1)
        named = jnp.zeros((rows, 128), F32)
        weight = jnp.zeros((rows, 128), F32)
        for k in range(ids_ref.shape[1]):
            hit = ids_ref[:, k : k + 1] == lane
            named = jnp.where(hit, 1.0, named)
            weight = jnp.where(hit, w_ref[:, k : k + 1], weight)
        named_t = named.T
        weight_t = weight.T
        earlier = jnp.where(iota((rows, rows), 0) < iota((rows, rows), 1), 1.0, 0.0).astype(BF)
        place = jnp.dot(named_t.astype(BF), earlier, preferred_element_type=F32)
        code = jnp.where(named_t > 0, place + 1.0, 0.0)
        r = iota((PACK, 1), 0) % ROWS
        slot = (r % CAP + 1).astype(F32)
        is_tok = r < CAP
        for e in range(N_Z):
            block = pl.ds(e * PACK, PACK)
            picked = jnp.where(jnp.broadcast_to(code[e : e + 1, :], (PACK, rows)) == slot, 1.0, 0.0)
            weighted = picked * jnp.broadcast_to(weight_t[e : e + 1, :], (PACK, rows))
            tok_sel = jnp.where(is_tok, picked, 0.0)
            cot_sel = jnp.where(is_tok, 0.0, picked)
            sel_ref[block, :rows] = tok_sel.astype(BF)
            sel_ref[block, rows:] = cot_sel.astype(BF)
            tab_ref[block, :rows] = jnp.where(is_tok, weighted, 0.0).astype(BF)
            tab_ref[block, rows:] = cot_sel.astype(BF)
            scale = jnp.sum(weighted, axis=1, keepdims=True)
            row_ref[block, :] = jnp.broadcast_to(jnp.where(is_tok, 1.0, scale), (PACK, 128))

    @pl.when(q == 0)
    def _():
        acc_ref[...] = jnp.zeros_like(acc_ref)

    total = N_Z * PACK
    here = (iota((total, 1), 0) % PACK) // ROWS == q
    sel = jnp.where(here, sel_ref[...], jnp.zeros((), BF))
    values = jnp.concatenate([tok_ref[...], cot_ref[...]], axis=0)
    acc_ref[...] += jnp.dot(sel, values, preferred_element_type=F32)

    @pl.when(q == N_X - 1)
    def _():
        send = (acc_ref[...] * row_ref[:, :1]).astype(BF)
        send_ref[...] = send.reshape(send_ref.shape)


def select(ids, weights, tokens, cotangent):
    rows, width = tokens.shape
    seg = width // (N_X * N_C)
    total = N_Z * PACK
    return pl.pallas_call(
        select_kernel,
        grid=(N_C, N_X),
        in_specs=[
            pl.BlockSpec(ids.shape, lambda c, q: (0, 0)),
            pl.BlockSpec(weights.shape, lambda c, q: (0, 0)),
            pl.BlockSpec((rows, seg), lambda c, q: (0, q * N_C + c)),
            pl.BlockSpec((rows, seg), lambda c, q: (0, q * N_C + c)),
        ],
        out_specs=[
            pl.BlockSpec((N_Z, 1, PACK, seg), lambda c, q: (0, c, 0, 0)),
            pl.BlockSpec((total, 2 * rows), lambda c, q: (0, 0)),
        ],
        out_shape=[
            jax.ShapeDtypeStruct((N_Z, N_C, PACK, seg), BF),
            jax.ShapeDtypeStruct((total, 2 * rows), BF),
        ],
        scratch_shapes=[
            pltpu.VMEM((total, 2 * rows), BF),
            pltpu.VMEM((total, 128), F32),
            pltpu.VMEM((total, seg), F32),
        ],
        compiler_params=pltpu.CompilerParams(vmem_limit_bytes=32 << 20),
        name="select_rows",
    )(ids, weights, tokens, cotangent)


HALF = N_Z * PACK
HROWS = N_Z * CAP


def unpack_kernel(in_ref, tok_ref, cot_ref):
    q = pl.program_id(1)
    shape = (2 * HROWS, HALF)
    row, col = iota(shape, 0), iota(shape, 1)
    is_cot = (row >= HROWS).astype(jnp.int32)
    place = row - is_cot * HROWS
    want = (place // CAP) * PACK + q * ROWS + is_cot * CAP + place % CAP
    perm = jnp.where(col == want, 1.0, 0.0).astype(BF)
    out = jnp.dot(perm, in_ref[...].reshape(HALF, -1), preferred_element_type=F32).astype(BF)
    tok_ref[...] = out[:HROWS]
    cot_ref[...] = out[HROWS:]


def unpack(packed):
    seg = packed.shape[2]
    out = jax.ShapeDtypeStruct((N_C * HROWS, N_X * seg), BF)
    return pl.pallas_call(
        unpack_kernel,
        grid=(2, N_X),
        in_specs=[pl.BlockSpec((N_Z, PACK, seg), lambda h, q: (h, 0, 0))],
        out_specs=[pl.BlockSpec((HROWS, seg), lambda h, q: (h, q))] * 2,
        out_shape=[out, out],
        compiler_params=pltpu.CompilerParams(vmem_limit_bytes=32 << 20),
        name="unpack_rows",
    )(packed)


def pack_kernel(out_ref, in_ref, send_ref, acc_ref):
    q = pl.program_id(1)

    @pl.when(q == 0)
    def _():
        acc_ref[...] = jnp.zeros_like(acc_ref)

    shape = (HALF, 2 * HROWS)
    row, col = iota(shape, 0), iota(shape, 1)
    r = row % ROWS
    is_cot = (r >= CAP).astype(jnp.int32)
    want = is_cot * HROWS + (row // PACK) * CAP + r - is_cot * CAP
    hit = (col == want) & ((row % PACK) // ROWS == q)
    perm = jnp.where(hit, 1.0, 0.0).astype(BF)
    values = jnp.concatenate([out_ref[...], in_ref[...]], axis=0)
    acc_ref[...] += jnp.dot(perm, values, preferred_element_type=F32)

    @pl.when(q == N_X - 1)
    def _():
        send_ref[...] = acc_ref[...].astype(BF).reshape(send_ref.shape)


def pack(out_rows, in_rows):
    seg = out_rows.shape[1] // N_X
    return pl.pallas_call(
        pack_kernel,
        grid=(2, N_X),
        in_specs=[pl.BlockSpec((HROWS, seg), lambda h, q: (h, q))] * 2,
        out_specs=pl.BlockSpec((N_Z, PACK, seg), lambda h, q: (h, 0, 0)),
        out_shape=jax.ShapeDtypeStruct((2 * N_Z, PACK, seg), BF),
        scratch_shapes=[pltpu.VMEM((HALF, seg), F32)],
        compiler_params=pltpu.CompilerParams(vmem_limit_bytes=32 << 20),
        name="pack_rows",
    )(out_rows, in_rows)


def combine_kernel(tab_ref, back_ref, out_ref, grad_ref):
    q = pl.program_id(1)
    total = N_Z * PACK
    here = (iota((total, 1), 0) % PACK) // ROWS == q
    tab = jnp.where(here, tab_ref[...], jnp.zeros((), BF))
    merged = lax.dot_general(
        tab,
        back_ref[...].reshape(total, -1),
        (((0,), (0,)), ((), ())),
        preferred_element_type=F32,
    ).astype(BF)
    rows = out_ref.shape[0]
    out_ref[...] = merged[:rows]
    grad_ref[...] = merged[rows:]


def combine(tab, back):
    seg = back.shape[2]
    rows = tab.shape[1] // 2
    out = jax.ShapeDtypeStruct((rows, N_X * N_C * seg), BF)
    return pl.pallas_call(
        combine_kernel,
        grid=(N_C, N_X),
        in_specs=[
            pl.BlockSpec(tab.shape, lambda c, q: (0, 0)),
            pl.BlockSpec((N_Z, 1, PACK, seg), lambda c, q: (0, c, 0, 0)),
        ],
        out_specs=[pl.BlockSpec((rows, seg), lambda c, q: (0, q * N_C + c))] * 2,
        out_shape=[out, out],
        compiler_params=pltpu.CompilerParams(vmem_limit_bytes=32 << 20),
        name="combine_rows",
    )(tab, back.reshape(N_Z, N_C, PACK, seg))


def dot_nn(a, b):
    return jnp.dot(a, b, preferred_element_type=F32)


def dot_nt(a, b):
    return lax.dot_general(a, b, (((1,), (1,)), ((), ())), preferred_element_type=F32)


def dot_tn(a, b):
    return lax.dot_general(a, b, (((0,), (0,)), ((), ())), preferred_element_type=F32)


def gather_y(rows):
    return lax.all_gather(rows, "y", axis=0, tiled=True)


def scatter_y(rows):
    return lax.psum_scatter(rows, "y", scatter_dimension=0, tiled=True)


def exchange(blocks):
    return lax.all_to_all(blocks, ("z", "c"), split_axis=0, concat_axis=0, tiled=True)


def local(tokens, cotangent, route_ids, router_weights, master, accumulator):
    quarter, cols = master.shape[1], master.shape[2]
    hid = cols // 3
    seg = quarter // N_C
    core = lax.axis_index("c")

    mine = master[0].astype(BF)
    keep = lax.dynamic_slice_in_dim(mine, core * seg, seg, 0)
    give = lax.dynamic_slice_in_dim(mine, (1 - core) * seg, seg, 0)
    pair = jnp.concatenate([keep, swap_core(give)], axis=1)
    weights = lax.all_gather(pair, "x", axis=0, tiled=True)

    send, tab = select(route_ids, router_weights, tokens, cotangent)
    packed = exchange(send.reshape(N_Z * N_C, PACK, seg))
    tok_part, cot_part = unpack(packed)
    in_rows = gather_y(tok_part)
    cot_rows = gather_y(cot_part)

    gate_up = jnp.concatenate([weights[:, : 2 * hid], weights[:, cols : cols + 2 * hid]], axis=1)
    down = jnp.concatenate([weights[:, 2 * hid : cols], weights[:, cols + 2 * hid :]], axis=1)
    pre_half = dot_nn(in_rows, gate_up)
    grad_half = dot_nn(cot_rows, down)

    def sum_cores(half):
        other = swap_core(half)
        mid = half.shape[1] // 2
        return half + jnp.concatenate([other[:, mid:], other[:, :mid]], axis=1)

    pre = sum_cores(pre_half).reshape(-1, 2, 2, hid)
    grad_hidden = sum_cores(grad_half).reshape(-1, 2, hid)
    gate_pre, up_pre = pre[:, :, 0], pre[:, :, 1]
    sig = jax.nn.sigmoid(gate_pre)
    silu = gate_pre * sig
    hidden = (silu * up_pre).astype(BF)
    grad_gate = grad_hidden * up_pre * sig * (1.0 + gate_pre * (1.0 - sig))
    grad_up = grad_hidden * silu
    grad_pre = jnp.stack([grad_gate, grad_up], axis=2).astype(BF)
    hidden = hidden.reshape(-1, 2 * hid)
    grad_pre = grad_pre.reshape(-1, 4 * hid)

    out_part = dot_nt(hidden, down).astype(BF)
    in_part = dot_nt(grad_pre, gate_up).astype(BF)
    back = exchange(pack(scatter_y(out_part), scatter_y(in_part)))
    output, input_grad = combine(tab, back)

    grad_gu = dot_tn(in_rows, grad_pre).astype(BF)
    grad_dn = dot_tn(cot_rows, hidden).astype(BF)
    full = jnp.concatenate(
        [grad_gu[:, : 2 * hid], grad_dn[:, :hid], grad_gu[:, 2 * hid :], grad_dn[:, hid:]], axis=1
    )
    summed = lax.psum_scatter(full, "x", scatter_dimension=0, tiled=True)
    here, there = summed[:, :cols], swap_core(summed[:, cols:])
    grad = jnp.where(
        core == 0,
        jnp.concatenate([here, there], axis=0),
        jnp.concatenate([there, here], axis=0),
    )
    grad = grad.astype(F32).reshape(quarter, 3, hid)
    accumulator_out = accumulator[0] + jnp.mean(grad * grad, axis=2).T
    scale = 1.0 / (jnp.sqrt(accumulator_out) + EPSILON)
    update = grad * scale.T[:, :, None]
    master_new = master[0] - LEARN_RATE * update.reshape(quarter, cols)
    returned = swap_core(master_new.astype(BF))
    return output, input_grad, returned[None], accumulator_out[None]


def solution(mesh):
    fine = Mesh(mesh.devices.reshape(N_X, N_Z, N_Y, N_C), ("x", "z", "y", "c"))
    rows = P(("x", "z", "y", "c"), None)
    weights = P(("z", "y", "c"), "x", None)
    sums = P(("z", "y", "c"), None, "x")
    return jax.shard_map(
        local,
        mesh=fine,
        in_specs=(rows, rows, rows, rows, weights, sums),
        out_specs=(rows, rows, weights, sums),
        check_vma=False,
    )
```

```python
import functools

import jax
import jax.numpy as jnp
from jax import lax
from jax.experimental import pallas as pl
from jax.experimental.pallas import tpu as pltpu
from jax.sharding import Mesh, PartitionSpec as P


N_X, N_Z, N_Y, N_C = 4, 8, 4, 2
CAP = 5
LEARN_RATE = 0.01
EPSILON = 1e-06
BF = jnp.bfloat16
F32 = jnp.float32
BLK = 256
VMEM = pl.BlockSpec(memory_space=pltpu.VMEM)


def swap_core(a):
    return lax.ppermute(a, "c", [(0, 1), (1, 0)])


def shift(a, axis, step):
    n = lax.axis_size(axis)
    return lax.ppermute(a, axis, [(i, (i + step) % n) for i in range(n)])


def iota(shape, dim):
    return lax.broadcasted_iota(jnp.int32, shape, dim)


def params(mib, **kw):
    return pltpu.CompilerParams(vmem_limit_bytes=mib << 20, **kw)


def like(*shape, dtype=BF):
    return jax.ShapeDtypeStruct(shape, dtype)


def dot_nn(a, b):
    return jnp.dot(a, b, preferred_element_type=F32)


def dot_nt(a, b):
    return lax.dot_general(a, b, (((1,), (1,)), ((), ())), preferred_element_type=F32)


def dot_tn(a, b):
    return lax.dot_general(a, b, (((0,), (0,)), ((), ())), preferred_element_type=F32)


def cost(flops, bytes_accessed):
    return pl.CostEstimate(flops=flops, bytes_accessed=bytes_accessed, transcendentals=0)


def select_kernel(scaled, with_tab, x_ref, ids_ref, w_ref, *refs):
    del x_ref
    segs, refs = refs[:N_X], refs[N_X:]
    send_ref, refs = refs[0], refs[1:]
    if with_tab:
        (out_tab, in_tab), refs = refs[:2], refs[2:]
    sel_ref, row_ref = refs
    tok = ids_ref.shape[0]
    packed = send_ref.shape[2]
    blocks = packed // CAP

    @pl.when(pl.program_id(0) == 0)
    def _():
        lane = iota((tok, 128), 1)
        named = jnp.zeros((tok, 128), F32)
        weight = jnp.zeros((tok, 128), F32)
        for k in range(ids_ref.shape[1]):
            hit = ids_ref[:, k : k + 1] == lane
            named = jnp.where(hit, 1.0, named)
            weight = jnp.where(hit, w_ref[:, k : k + 1], weight)
        earlier = jnp.where(iota((tok, tok), 1) < iota((tok, tok), 0), 1.0, 0.0).astype(BF)
        place = dot_nn(earlier, named.astype(BF))
        code = jnp.where(named > 0, place + 1.0, 0.0)
        code_t = code.T
        weight_t = weight.T
        r = iota((packed, 1), 0)
        slot = (r % CAP + 1).astype(F32)
        shape = (packed, blocks * tok)
        diag = iota(shape, 0) // CAP == iota(shape, 1) // tok
        for e in range(N_Z):
            block = pl.ds(e * packed, packed)
            picked = jnp.broadcast_to(code_t[e : e + 1, :], (packed, tok)) == slot
            ones = jnp.where(picked, 1.0, 0.0)
            wide = jnp.concatenate([ones] * blocks, axis=1)
            sel_ref[block, :] = jnp.where(diag, wide, 0.0).astype(BF)
            if scaled:
                part = jnp.where(picked, jnp.broadcast_to(weight_t[e : e + 1, :], (packed, tok)), 0.0)
                row_ref[block, :] = jnp.broadcast_to(jnp.sum(part, axis=1, keepdims=True), (packed, 128))
        if with_tab:
            total = N_Z * packed
            l = iota((128, total), 1)
            spread = jnp.where(l // packed == iota((128, total), 0), 1.0, 0.0).astype(BF)
            l = iota((tok, total), 1) % packed
            valid = (dot_nn(code.astype(BF), spread) == (l % CAP + 1).astype(F32)) & (l < blocks * CAP)
            in_tab[...] = jnp.where(valid, 1.0, 0.0).astype(BF)
            out_tab[...] = jnp.where(valid, dot_nn(weight.astype(BF), spread), 0.0).astype(BF)

    wide = jnp.concatenate([s[...] for s in segs], axis=1)
    stack = jnp.concatenate([wide[:, q * BLK : (q + 1) * BLK] for q in range(blocks)], axis=0)
    rows = dot_nn(sel_ref[...], stack)
    if scaled:
        rows = rows * row_ref[:, :1]
    send_ref[...] = rows.astype(BF).reshape(send_ref.shape)


def packed_rows(width):
    blocks = width // N_C // BLK
    return -(-blocks * CAP // 8) * 8


def select(x, ids, weights, data, scaled, with_tab):
    tok, width = data.shape
    seg = width // (N_X * N_C)
    packed = packed_rows(width)
    blocks = packed // CAP
    total = N_Z * packed
    seg_spec = lambda k: pl.BlockSpec(
        (tok, seg), lambda c, x: (0, lax.rem(x[0] + k, N_X) * N_C + c)
    )
    out_specs = [pl.BlockSpec((N_Z, 1, packed, BLK), lambda c, x: (0, c, 0, 0))]
    out_shape = [like(N_Z, N_C, packed, BLK)]
    if with_tab:
        out_specs += [pl.BlockSpec((tok, total), lambda c, x: (0, 0))] * 2
        out_shape += [like(tok, total)] * 2
    return pl.pallas_call(
        functools.partial(select_kernel, scaled, with_tab),
        grid_spec=pltpu.PrefetchScalarGridSpec(
            num_scalar_prefetch=1,
            grid=(N_C,),
            in_specs=[
                pl.BlockSpec(ids.shape, lambda c, x: (0, 0)),
                pl.BlockSpec(weights.shape, lambda c, x: (0, 0)),
            ]
            + [seg_spec(k) for k in range(N_X)],
            out_specs=out_specs,
            scratch_shapes=[
                pltpu.VMEM((total, blocks * tok), BF),
                pltpu.VMEM((total, 128), F32),
            ],
        ),
        out_shape=out_shape,
        compiler_params=params(32),
        cost_estimate=cost(2 * N_C * total * blocks * tok * BLK, 4 * tok * width),
        name="select_cot" if scaled else "select_tok",
    )(x, ids, weights, *([data] * N_X))


GROWS = N_Z * CAP


def unpack_kernel(in_ref, a_ref, b_ref):
    packed = in_ref.shape[1]
    blocks = packed // CAP
    shape = (blocks * GROWS, N_Z * packed)
    row, col = iota(shape, 0), iota(shape, 1)
    place = row % GROWS
    want = place // CAP * packed + row // GROWS * CAP + place % CAP
    perm = jnp.where(col == want, 1.0, 0.0).astype(BF)
    out = dot_nn(perm, in_ref[...].reshape(N_Z * packed, BLK))
    half = blocks // 2
    for q in range(blocks):
        ref = a_ref if q < half else b_ref
        ref[:, pl.ds(q % half * BLK, BLK)] = out[q * GROWS : (q + 1) * GROWS].astype(BF)


def unpack(packed):
    srcs, rows, _ = packed.shape
    half = rows // CAP * BLK // 2
    out = like(srcs * CAP, half)
    return pl.pallas_call(
        unpack_kernel,
        grid=(srcs // N_Z,),
        in_specs=[pl.BlockSpec((N_Z, rows, BLK), lambda h: (h, 0, 0))],
        out_specs=[pl.BlockSpec((GROWS, half), lambda h: (h, 0))] * 2,
        out_shape=[out, out],
        compiler_params=params(16),
        cost_estimate=cost(1 << 29, 1 << 21),
        name="unpack_rows",
    )(packed)


def pack_kernel(*refs):
    *parts, send_ref = refs
    packed = send_ref.shape[1]
    blocks = packed // CAP
    half = blocks // 2
    total = [sum(r[...].astype(F32) for r in parts[i::2]) for i in range(2)]
    stack = jnp.concatenate(
        [total[q // half][:, q % half * BLK : (q % half + 1) * BLK] for q in range(blocks)], axis=0
    ).astype(BF)
    shape = (N_Z * packed, blocks * GROWS)
    row, col = iota(shape, 0), iota(shape, 1)
    r = row % packed
    want = r // CAP * GROWS + row // packed * CAP + r % CAP
    perm = jnp.where((col == want) & (r < blocks * CAP), 1.0, 0.0).astype(BF)
    send_ref[...] = dot_nn(perm, stack).astype(BF).reshape(send_ref.shape)


def pack(*parts):
    rows, half = parts[0].shape
    packed = packed_rows(half * 2 * N_C)
    return pl.pallas_call(
        pack_kernel,
        grid=(rows // GROWS,),
        in_specs=[pl.BlockSpec((GROWS, half), lambda h: (h, 0))] * len(parts),
        out_specs=pl.BlockSpec((N_Z, packed, BLK), lambda h: (h, 0, 0)),
        out_shape=like(rows // CAP, packed, BLK),
        compiler_params=params(16),
        cost_estimate=cost(1 << 29, 1 << 22),
        name="pack_rows",
    )(*parts)


def combine_kernel(x_ref, tab_ref, back_ref, out_ref, big_ref, acc_ref):
    del x_ref
    c, k = pl.program_id(0), pl.program_id(1)
    tok, total = tab_ref.shape
    packed = back_ref.shape[2]
    blocks = packed // CAP
    seg = out_ref.shape[1]

    @pl.when((c == 0) & (k == 0))
    def _():
        where = iota((tok, total), 1) % packed // CAP
        for q in range(blocks):
            big_ref[pl.ds(q * tok, tok), :] = jnp.where(where == q, tab_ref[...], jnp.zeros((), BF))

    @pl.when(k == 0)
    def _():
        out = dot_nn(big_ref[...], back_ref[...].reshape(total, BLK)).astype(BF)
        for q in range(blocks):
            acc_ref[:, pl.ds(q * BLK, BLK)] = out[q * tok : (q + 1) * tok]

    for j in range(N_X):

        @pl.when(k == j)
        def _(j=j):
            out_ref[...] = acc_ref[:, pl.ds(j * seg, seg)]


def combine(x, tab, back):
    tok, total = tab.shape
    _, packed, _ = back.shape
    width = packed // CAP * BLK * N_C
    seg = width // (N_X * N_C)
    return pl.pallas_call(
        combine_kernel,
        grid_spec=pltpu.PrefetchScalarGridSpec(
            num_scalar_prefetch=1,
            grid=(N_C, N_X),
            in_specs=[
                pl.BlockSpec((tok, total), lambda c, k, x: (0, 0)),
                pl.BlockSpec((N_Z, 1, packed, BLK), lambda c, k, x: (0, c, 0, 0)),
            ],
            out_specs=pl.BlockSpec(
                (tok, seg), lambda c, k, x: (0, lax.rem(x[0] + k, N_X) * N_C + c)
            ),
            scratch_shapes=[
                pltpu.VMEM((packed // CAP * tok, total), BF),
                pltpu.VMEM((tok, width // N_C), BF),
            ],
        ),
        out_shape=like(tok, width),
        compiler_params=params(24),
        cost_estimate=cost(1 << 30, 1 << 22),
        name="combine_rows",
    )(x, tab, back.reshape(N_Z, N_C, packed, BLK))


def ring_gather(a, b, axis):
    a3, b1 = shift(a, axis, 1), shift(b, axis, -1)
    b3, a1 = shift(b, axis, 1), shift(a, axis, -1)
    a2, b2 = shift(a3, axis, 1), shift(b1, axis, -1)
    return [(a, b), (a1, b1), (a2, b2), (a3, b3)]


def ring_scatter(pieces, axis):
    (a0, b0), (a1, b1), (a2, b2), (a3, b3) = pieces
    ra, rb = shift(a2, axis, 1), shift(b2, axis, -1)
    far_b, far_a = shift(b1, axis, 1), shift(a3, axis, -1)
    near_a = shift((a1.astype(F32) + ra.astype(F32)).astype(BF), axis, 1)
    near_b = shift((b3.astype(F32) + rb.astype(F32)).astype(BF), axis, -1)
    return a0, b0, far_a, far_b, near_a, near_b


def flat(pairs):
    return [half for pair in pairs for half in pair]


def segment(rows, k, seg):
    half = k // 2
    cols = pl.ds(k % 2 * seg, seg)
    return jnp.concatenate([rows[2 * i + half][:, cols] for i in range(N_Y)], axis=0)


def project_kernel(lo, hi, *refs):
    rows, w, out_ref = refs[: 2 * N_Y], refs[2 * N_Y : -1], refs[-1]
    seg = w[0].shape[0]
    acc = None
    for k in range(N_X):
        both = jnp.concatenate([w[2 * k][:, lo:hi], w[2 * k + 1][:, lo:hi]], axis=1)
        part = dot_nn(segment(rows, k, seg), both)
        acc = part if acc is None else acc + part
    out_ref[...] = acc


def project(rows, weights, lo, hi):
    count = rows[0][0].shape[0] * N_Y
    seg, cols = weights[0][0].shape
    return pl.pallas_call(
        functools.partial(project_kernel, lo, hi),
        in_specs=[VMEM] * (2 * N_Y + 2 * N_X),
        out_specs=VMEM,
        out_shape=like(count, 2 * (hi - lo), dtype=F32),
        compiler_params=params(24),
        cost_estimate=cost(4 * count * seg * N_X * (hi - lo), 8 << 20),
        name="project_rows",
    )(*flat(rows), *flat(weights))


def sum_cores(half, other):
    mid = half.shape[1] // 2
    return half[...] + jnp.concatenate([other[:, mid:], other[:, :mid]], axis=1)


def spread_back(value, w, lo, hi, outs):
    seg = w[0].shape[0]
    chunk = value.shape[0] // N_Y
    for k in range(N_X):
        both = jnp.concatenate([w[2 * k][:, lo:hi], w[2 * k + 1][:, lo:hi]], axis=1)
        part = dot_nt(value, both).astype(BF)
        for i in range(N_Y):
            outs[2 * i + k // 2][:, pl.ds(k % 2 * seg, seg)] = part[i * chunk : (i + 1) * chunk]


def forward_kernel(hid, half_ref, other_ref, *refs):
    w, hidden_ref, outs = refs[: 2 * N_X], refs[2 * N_X], refs[2 * N_X + 1 :]
    pre = sum_cores(half_ref, other_ref)
    parts = []
    for s in range(2):
        gate = pre[:, 2 * s * hid : (2 * s + 1) * hid]
        up = pre[:, (2 * s + 1) * hid : (2 * s + 2) * hid]
        parts.append(gate * jax.nn.sigmoid(gate) * up)
    hidden = jnp.concatenate(parts, axis=1).astype(BF)
    hidden_ref[...] = hidden
    spread_back(hidden, w, 2 * hid, 3 * hid, outs)


def backward_kernel(hid, half_ref, other_ref, ghalf_ref, gother_ref, *refs):
    w, grad_ref, outs = refs[: 2 * N_X], refs[2 * N_X], refs[2 * N_X + 1 :]
    pre = sum_cores(half_ref, other_ref)
    grad_hidden = sum_cores(ghalf_ref, gother_ref)
    parts = []
    for s in range(2):
        gate = pre[:, 2 * s * hid : (2 * s + 1) * hid]
        up = pre[:, (2 * s + 1) * hid : (2 * s + 2) * hid]
        grad = grad_hidden[:, s * hid : (s + 1) * hid]
        sig = jax.nn.sigmoid(gate)
        parts += [grad * up * sig * (1.0 + gate * (1.0 - sig)), grad * (gate * sig)]
    grad_pre = jnp.concatenate(parts, axis=1).astype(BF)
    grad_ref[...] = grad_pre
    spread_back(grad_pre, w, 0, 2 * hid, outs)


def middle(kernel, name, halves, weights, out_cols):
    count = halves[0].shape[0]
    seg, cols = weights[0][0].shape
    outs = [like(count, out_cols)] + [like(count // N_Y, 2 * seg)] * (2 * N_Y)
    first, *pieces = pl.pallas_call(
        functools.partial(kernel, cols // 3),
        in_specs=[VMEM] * (len(halves) + 2 * N_X),
        out_specs=[VMEM] * len(outs),
        out_shape=outs,
        compiler_params=params(32),
        cost_estimate=cost(2 * count * seg * N_X * out_cols, 8 << 20),
        name=name,
    )(*halves, *flat(weights))
    return first, list(zip(pieces[::2], pieces[1::2]))


def weight_grad_kernel(ks, hid, hidden_ref, grad_ref, *refs):
    tok, cot, outs = refs[: 2 * N_Y], refs[2 * N_Y : 4 * N_Y], refs[4 * N_Y :]
    seg = outs[0].shape[0]
    for i, k in enumerate(ks):
        gate_up = dot_tn(segment(tok, k, seg), grad_ref[...]).astype(BF)
        down = dot_tn(segment(cot, k, seg), hidden_ref[...]).astype(BF)
        for s in range(2):
            outs[2 * i + s][:, : 2 * hid] = gate_up[:, 2 * s * hid : (2 * s + 2) * hid]
            outs[2 * i + s][:, 2 * hid :] = down[:, s * hid : (s + 1) * hid]


def weight_grad(ks, hidden, grad_pre, tok_rows, cot_rows):
    hid = hidden.shape[1] // 2
    seg = tok_rows[0][0].shape[1] // 2
    outs = pl.pallas_call(
        functools.partial(weight_grad_kernel, ks, hid),
        in_specs=[VMEM] * (2 + 4 * N_Y),
        out_specs=[VMEM] * (2 * len(ks)),
        out_shape=[like(seg, 3 * hid)] * (2 * len(ks)),
        compiler_params=params(32),
        cost_estimate=cost(2 * len(ks) * seg * 6 * hid * hidden.shape[0], 5 << 20),
        name="weight_grad",
    )(hidden, grad_pre, *flat(tok_rows), *flat(cot_rows))
    return list(zip(outs[::2], outs[1::2]))


def split_kernel(c_ref, keep_in, give_in, keep_ref, give_ref):
    del c_ref
    keep_ref[...] = keep_in[0].astype(BF)
    give_ref[...] = give_in[0].astype(BF)


def split_master(c, master):
    _, quarter, cols = master.shape
    seg = quarter // N_C
    out = like(seg, cols)
    return pl.pallas_call(
        split_kernel,
        grid_spec=pltpu.PrefetchScalarGridSpec(
            num_scalar_prefetch=1,
            grid=(1,),
            in_specs=[
                pl.BlockSpec((1, seg, cols), lambda i, c: (0, c[0], 0)),
                pl.BlockSpec((1, seg, cols), lambda i, c: (0, 1 - c[0], 0)),
            ],
            out_specs=[pl.BlockSpec((seg, cols), lambda i, c: (0, 0))] * 2,
        ),
        out_shape=[out, out],
        compiler_params=params(16),
        cost_estimate=cost(0, 5 << 20),
        name="split_master",
    )(c, master, master)


def update_kernel(c_ref, master_ref, sums_ref, other_ref, *refs):
    *parts, new_ref, out_ref, grad_ref = refs
    here = pl.program_id(0) == c_ref[0]

    @pl.when(here)
    def _():
        grad_ref[...] = sum(p[...].astype(F32) for p in parts).astype(BF).astype(F32)

    @pl.when(jnp.logical_not(here))
    def _():
        grad_ref[...] = other_ref[...].astype(F32)

    seg, cols = grad_ref.shape
    hid = cols // 3
    ones = jnp.ones((8, hid), F32)
    means = []
    for g in range(3):
        grad = grad_ref[:, g * hid : (g + 1) * hid]
        total = lax.dot_general(
            ones,
            grad * grad,
            (((1,), (1,)), ((), ())),
            precision=lax.Precision.HIGHEST,
            preferred_element_type=F32,
        )
        means.append(total[:1] / hid)
    sums = sums_ref[0] + jnp.concatenate(means, axis=0)
    out_ref[0] = sums
    scale = LEARN_RATE / (jnp.sqrt(sums) + EPSILON)
    tall = jnp.concatenate([scale, jnp.zeros((125, seg), F32)], axis=0).T
    for g in range(3):
        span = pl.ds(g * hid, hid)
        new_ref[:, span] = (master_ref[0, :, span] - grad_ref[:, span] * tall[:, g : g + 1]).astype(BF)


def update(c, master, sums, other, *parts):
    _, quarter, cols = master.shape
    seg = quarter // N_C
    piece = pl.BlockSpec((seg, cols), lambda h, c: (0, 0))
    rows = pl.BlockSpec((seg, cols), lambda h, c: (h, 0))
    lanes = pl.BlockSpec((1, 3, seg), lambda h, c: (0, 0, h))
    return pl.pallas_call(
        update_kernel,
        grid_spec=pltpu.PrefetchScalarGridSpec(
            num_scalar_prefetch=1,
            grid=(N_C,),
            in_specs=[pl.BlockSpec((1, seg, cols), lambda h, c: (0, h, 0)), lanes]
            + [piece] * (1 + len(parts)),
            out_specs=[rows, lanes],
            scratch_shapes=[pltpu.VMEM((seg, cols), F32)],
        ),
        out_shape=[like(quarter, cols), like(*sums.shape, dtype=F32)],
        compiler_params=params(24),
        cost_estimate=cost(0, 8 << 20),
        name="update_master",
    )(c, master, sums, other, *parts)


def exchange(blocks):
    return lax.all_to_all(blocks, ("z", "c"), split_axis=0, concat_axis=0, tiled=True)


def local(tokens, cotangent, route_ids, router_weights, master, accumulator):
    hid = master.shape[2] // 3
    x = lax.axis_index("x").reshape(1)
    core = lax.axis_index("c").reshape(1)

    tok_send, out_tab, in_tab = select(x, route_ids, router_weights, tokens, False, True)
    (cot_send,) = select(x, route_ids, router_weights, cotangent, True, False)
    merge = lambda a: a.reshape((N_Z * N_C,) + a.shape[2:])
    tok_packed = exchange(merge(tok_send))
    cot_packed = exchange(merge(cot_send))

    keep, give = split_master(core, master)
    weights = ring_gather(keep, swap_core(give), "x")

    tok_rows = ring_gather(*unpack(tok_packed), "y")
    cot_rows = ring_gather(*unpack(cot_packed), "y")

    pre = project(tok_rows, weights, 0, 2 * hid)
    pre_other = swap_core(pre)
    hidden, out_pieces = middle(forward_kernel, "forward_rows", (pre, pre_other), weights, 2 * hid)
    output = combine(x, out_tab, exchange(pack(*ring_scatter(out_pieces, "y"))))

    grad_hidden = project(cot_rows, weights, 2 * hid, 3 * hid)
    grad_other = swap_core(grad_hidden)
    grad_pre, in_pieces = middle(
        backward_kernel, "backward_rows", (pre, pre_other, grad_hidden, grad_other), weights, 4 * hid
    )
    input_grad = combine(x, in_tab, exchange(pack(*ring_scatter(in_pieces, "y"))))

    (far,) = weight_grad((2,), hidden, grad_pre, tok_rows, cot_rows)
    near, here, last = weight_grad((1, 0, 3), hidden, grad_pre, tok_rows, cot_rows)
    parts = ring_scatter([here, near, far, last], "x")
    got = sum(p.astype(F32) for p in parts[1::2]).astype(BF)
    new, sums = update(core, master, accumulator, swap_core(got), *parts[::2])
    return output, input_grad, swap_core(new)[None], sums


def solution(mesh):
    fine = Mesh(mesh.devices.reshape(N_X, N_Z, N_Y, N_C), ("x", "z", "y", "c"))
    rows = P(("x", "z", "y", "c"), None)
    weights = P(("z", "y", "c"), "x", None)
    sums = P(("z", "y", "c"), None, "x")
    return jax.shard_map(
        local,
        mesh=fine,
        in_specs=(rows, rows, rows, rows, weights, sums),
        out_specs=(rows, rows, weights, sums),
        check_vma=False,
    )
```

```python
import functools

import jax
import jax.numpy as jnp
from jax import lax
from jax.experimental import pallas as pl
from jax.experimental.pallas import tpu as pltpu
from jax.sharding import Mesh, PartitionSpec as P


N_X, N_Z, N_Y, N_C = 4, 8, 4, 2
CAP = 5
LEARN_RATE = 0.01
EPSILON = 1e-06
BF = jnp.bfloat16
F32 = jnp.float32
COST = 100
BLK = 256


def swap_core(a):
    return lax.ppermute(a, "c", [(0, 1), (1, 0)])


def shift(a, axis, step):
    n = lax.axis_size(axis)
    return lax.ppermute(a, axis, [(i, (i + step) % n) for i in range(n)])


def iota(shape, dim):
    return lax.broadcasted_iota(jnp.int32, shape, dim)


def params(mib, **kw):
    return pltpu.CompilerParams(vmem_limit_bytes=mib << 20, **kw)


def like(*shape, dtype=BF):
    return jax.ShapeDtypeStruct(shape, dtype)


def dot_nn(a, b):
    return jnp.dot(a, b, preferred_element_type=F32)


def dot_nt(a, b):
    return lax.dot_general(a, b, (((1,), (1,)), ((), ())), preferred_element_type=F32)


def dot_tn(a, b):
    return lax.dot_general(a, b, (((0,), (0,)), ((), ())), preferred_element_type=F32)


def cost(micros):
    return pl.CostEstimate(
        flops=micros * 10**9, bytes_accessed=micros * 10**6, transcendentals=0
    )


def select_kernel(scaled, with_tab, x_ref, ids_ref, w_ref, *refs):
    del x_ref
    segs, refs = refs[:N_X], refs[N_X:]
    send_ref, refs = refs[0], refs[1:]
    if with_tab:
        (out_tab, in_tab), refs = refs[:2], refs[2:]
    sel_ref, row_ref = refs
    tok = ids_ref.shape[0]
    packed = send_ref.shape[2]
    blocks = packed // CAP

    @pl.when(pl.program_id(0) == 0)
    def _():
        lane = iota((tok, 128), 1)
        named = jnp.zeros((tok, 128), F32)
        weight = jnp.zeros((tok, 128), F32)
        for k in range(ids_ref.shape[1]):
            hit = ids_ref[:, k : k + 1] == lane
            named = jnp.where(hit, 1.0, named)
            weight = jnp.where(hit, w_ref[:, k : k + 1], weight)
        earlier = jnp.where(iota((tok, tok), 1) < iota((tok, tok), 0), 1.0, 0.0).astype(BF)
        place = dot_nn(earlier, named.astype(BF))
        code = jnp.where(named > 0, place + 1.0, 0.0)
        code_t = code.T
        weight_t = weight.T
        r = iota((packed, 1), 0)
        slot = (r % CAP + 1).astype(F32)
        shape = (packed, blocks * tok)
        diag = iota(shape, 0) // CAP == iota(shape, 1) // tok
        for e in range(N_Z):
            block = pl.ds(e * packed, packed)
            picked = jnp.broadcast_to(code_t[e : e + 1, :], (packed, tok)) == slot
            ones = jnp.where(picked, 1.0, 0.0)
            wide = jnp.concatenate([ones] * blocks, axis=1)
            sel_ref[block, :] = jnp.where(diag, wide, 0.0).astype(BF)
            if scaled:
                part = jnp.where(picked, jnp.broadcast_to(weight_t[e : e + 1, :], (packed, tok)), 0.0)
                row_ref[block, :] = jnp.broadcast_to(jnp.sum(part, axis=1, keepdims=True), (packed, 128))
        if with_tab:
            total = N_Z * packed
            l = iota((128, total), 1)
            spread = jnp.where(l // packed == iota((128, total), 0), 1.0, 0.0).astype(BF)
            l = iota((tok, total), 1) % packed
            valid = (dot_nn(code.astype(BF), spread) == (l % CAP + 1).astype(F32)) & (l < blocks * CAP)
            in_tab[...] = jnp.where(valid, 1.0, 0.0).astype(BF)
            out_tab[...] = jnp.where(valid, dot_nn(weight.astype(BF), spread), 0.0).astype(BF)

    wide = jnp.concatenate([s[...] for s in segs], axis=1)
    stack = jnp.concatenate([wide[:, q * BLK : (q + 1) * BLK] for q in range(blocks)], axis=0)
    rows = dot_nn(sel_ref[...], stack)
    if scaled:
        rows = rows * row_ref[:, :1]
    send_ref[...] = rows.astype(BF).reshape(send_ref.shape)


def packed_rows(width):
    blocks = width // N_C // BLK
    return -(-blocks * CAP // 8) * 8


def select(x, ids, weights, data, scaled, with_tab):
    tok, width = data.shape
    seg = width // (N_X * N_C)
    packed = packed_rows(width)
    blocks = packed // CAP
    total = N_Z * packed
    seg_spec = lambda k: pl.BlockSpec(
        (tok, seg), lambda c, x: (0, lax.rem(x[0] + k, N_X) * N_C + c)
    )
    out_specs = [pl.BlockSpec((N_Z, 1, packed, BLK), lambda c, x: (0, c, 0, 0))]
    out_shape = [like(N_Z, N_C, packed, BLK)]
    if with_tab:
        out_specs += [pl.BlockSpec((tok, total), lambda c, x: (0, 0))] * 2
        out_shape += [like(tok, total)] * 2
    return pl.pallas_call(
        functools.partial(select_kernel, scaled, with_tab),
        grid_spec=pltpu.PrefetchScalarGridSpec(
            num_scalar_prefetch=1,
            grid=(N_C,),
            in_specs=[
                pl.BlockSpec(ids.shape, lambda c, x: (0, 0)),
                pl.BlockSpec(weights.shape, lambda c, x: (0, 0)),
            ]
            + [seg_spec(k) for k in range(N_X)],
            out_specs=out_specs,
            scratch_shapes=[
                pltpu.VMEM((total, blocks * tok), BF),
                pltpu.VMEM((total, 128), F32),
            ],
        ),
        out_shape=out_shape,
        compiler_params=params(32),
        cost_estimate=cost(COST),
        name="select_cot" if scaled else "select_tok",
    )(x, ids, weights, *([data] * N_X))


GROWS = N_Z * CAP


def unpack_kernel(in_ref, out_ref):
    packed = in_ref.shape[1]
    blocks = packed // CAP
    shape = (blocks * GROWS, N_Z * packed)
    row, col = iota(shape, 0), iota(shape, 1)
    place = row % GROWS
    want = place // CAP * packed + row // GROWS * CAP + place % CAP
    perm = jnp.where(col == want, 1.0, 0.0).astype(BF)
    out = dot_nn(perm, in_ref[...].reshape(N_Z * packed, BLK))
    for q in range(blocks):
        out_ref[:, pl.ds(q * BLK, BLK)] = out[q * GROWS : (q + 1) * GROWS].astype(BF)


def unpack(packed):
    srcs, rows, _ = packed.shape
    width = rows // CAP * BLK
    return pl.pallas_call(
        unpack_kernel,
        grid=(srcs // N_Z,),
        in_specs=[pl.BlockSpec((N_Z, rows, BLK), lambda h: (h, 0, 0))],
        out_specs=pl.BlockSpec((GROWS, width), lambda h: (h, 0)),
        out_shape=like(srcs * CAP, width),
        compiler_params=params(16),
        cost_estimate=cost(COST),
        name="unpack_rows",
    )(packed)


def pack_kernel(*refs):
    *parts, send_ref = refs
    packed = send_ref.shape[1]
    blocks = packed // CAP
    total = sum(r[...].astype(F32) for r in parts)
    stack = jnp.concatenate(
        [total[:, q * BLK : (q + 1) * BLK] for q in range(blocks)], axis=0
    ).astype(BF)
    shape = (N_Z * packed, blocks * GROWS)
    row, col = iota(shape, 0), iota(shape, 1)
    r = row % packed
    want = r // CAP * GROWS + row // packed * CAP + r % CAP
    perm = jnp.where((col == want) & (r < blocks * CAP), 1.0, 0.0).astype(BF)
    send_ref[...] = dot_nn(perm, stack).astype(BF).reshape(send_ref.shape)


def pack(*parts):
    rows, width = parts[0].shape
    packed = packed_rows(width * N_C)
    return pl.pallas_call(
        pack_kernel,
        grid=(rows // GROWS,),
        in_specs=[pl.BlockSpec((GROWS, width), lambda h: (h, 0))] * len(parts),
        out_specs=pl.BlockSpec((N_Z, packed, BLK), lambda h: (h, 0, 0)),
        out_shape=like(rows // CAP, packed, BLK),
        compiler_params=params(16),
        cost_estimate=cost(COST),
        name="pack_rows",
    )(*parts)


def combine_kernel(x_ref, tab_ref, back_ref, out_ref, big_ref, acc_ref):
    del x_ref
    c, k = pl.program_id(0), pl.program_id(1)
    tok, total = tab_ref.shape
    packed = back_ref.shape[2]
    blocks = packed // CAP
    seg = out_ref.shape[1]

    @pl.when((c == 0) & (k == 0))
    def _():
        where = iota((tok, total), 1) % packed // CAP
        for q in range(blocks):
            big_ref[pl.ds(q * tok, tok), :] = jnp.where(where == q, tab_ref[...], jnp.zeros((), BF))

    @pl.when(k == 0)
    def _():
        out = dot_nn(big_ref[...], back_ref[...].reshape(total, BLK)).astype(BF)
        for q in range(blocks):
            acc_ref[:, pl.ds(q * BLK, BLK)] = out[q * tok : (q + 1) * tok]

    for j in range(N_X):

        @pl.when(k == j)
        def _(j=j):
            out_ref[...] = acc_ref[:, pl.ds(j * seg, seg)]


def combine(x, tab, back):
    tok, total = tab.shape
    _, packed, _ = back.shape
    width = packed // CAP * BLK * N_C
    seg = width // (N_X * N_C)
    return pl.pallas_call(
        combine_kernel,
        grid_spec=pltpu.PrefetchScalarGridSpec(
            num_scalar_prefetch=1,
            grid=(N_C, N_X),
            in_specs=[
                pl.BlockSpec((tok, total), lambda c, k, x: (0, 0)),
                pl.BlockSpec((N_Z, 1, packed, BLK), lambda c, k, x: (0, c, 0, 0)),
            ],
            out_specs=pl.BlockSpec(
                (tok, seg), lambda c, k, x: (0, lax.rem(x[0] + k, N_X) * N_C + c)
            ),
            scratch_shapes=[
                pltpu.VMEM((packed // CAP * tok, total), BF),
                pltpu.VMEM((tok, width // N_C), BF),
            ],
        ),
        out_shape=like(tok, width),
        compiler_params=params(24),
        cost_estimate=cost(COST),
        name="combine_rows",
    )(x, tab, back.reshape(N_Z, N_C, packed, BLK))


def ring_gather(piece, axis, step):
    ahead, behind = shift(piece, axis, -1), shift(piece, axis, 1)
    far = shift(behind if step == 1 else ahead, axis, step)
    return [piece, ahead, far, behind]


def ring_scatter(pieces, axis, step):
    here, ahead, far, behind = pieces
    near, other = (ahead, behind) if step == 1 else (behind, ahead)
    passed = shift(far, axis, step)
    direct = shift(other, axis, -step)
    joint = shift((near.astype(F32) + passed.astype(F32)).astype(BF), axis, step)
    return here, direct, joint


ANY = pl.BlockSpec(memory_space=pl.ANY)


def stacked(rows):
    return jnp.concatenate([r[...] for r in rows], axis=0)


def fetch(weights, lo, hi, buf, sem):
    k = pl.program_id(0)

    @pl.when(k == 0)
    def _():
        for j, w in enumerate(weights):
            pltpu.make_async_copy(
                w.at[:, pl.ds(lo, hi - lo)], buf.at[j], sem.at[j]
            ).start()

    for s in range(2):
        j = 2 * k + s
        pltpu.make_async_copy(
            weights[0].at[:, pl.ds(lo, hi - lo)], buf.at[j], sem.at[j]
        ).wait()
    return jnp.concatenate([buf[2 * k], buf[2 * k + 1]], axis=1)


def fetch_scratch(weights, lo, hi):
    count = len(weights)
    return [
        pltpu.VMEM((count, weights[0].shape[0], hi - lo), BF),
        pltpu.SemaphoreType.DMA((count,)),
    ]


def row_specs(count, chunk, seg):
    return [pl.BlockSpec((chunk, seg), lambda k: (0, k))] * count


def whole(shape):
    return pl.BlockSpec(shape, lambda k: (0,) * len(shape))


def project_kernel(lo, hi, *refs):
    rows, weights, (out_ref, buf, sem) = refs[:N_Y], refs[N_Y:-3], refs[-3:]
    part = dot_nn(stacked(rows), fetch(weights, lo, hi, buf, sem))

    @pl.when(pl.program_id(0) == 0)
    def _():
        out_ref[...] = part

    @pl.when(pl.program_id(0) > 0)
    def _():
        out_ref[...] += part


def project(rows, weights, lo, hi):
    chunk = rows[0].shape[0]
    seg = weights[0].shape[0]
    shape = (chunk * N_Y, 2 * (hi - lo))
    return pl.pallas_call(
        functools.partial(project_kernel, lo, hi),
        grid=(N_X,),
        in_specs=row_specs(N_Y, chunk, seg) + [ANY] * len(weights),
        out_specs=whole(shape),
        out_shape=like(*shape, dtype=F32),
        scratch_shapes=fetch_scratch(weights, lo, hi),
        compiler_params=params(24),
        cost_estimate=cost(COST),
        name="project_rows",
    )(*rows, *weights)


def sum_cores(half, other):
    mid = half.shape[1] // 2
    return half[...] + jnp.concatenate([other[:, mid:], other[:, :mid]], axis=1)


def gates(pre, hid):
    for s in range(2):
        gate = pre[:, 2 * s * hid : (2 * s + 1) * hid]
        yield gate, pre[:, (2 * s + 1) * hid : (2 * s + 2) * hid], jax.nn.sigmoid(gate)


def spread_back(value_ref, weights, outs):
    part = lax.dot_general(
        value_ref[...], weights, (((1,), (1,)), ((), ())), preferred_element_type=F32
    ).astype(BF)
    chunk = part.shape[0] // N_Y
    for i in range(N_Y):
        outs[i][...] = part[i * chunk : (i + 1) * chunk]


def forward_kernel(lo, hi, half_ref, other_ref, *refs):
    weights, hidden_ref, outs, (buf, sem) = refs[:-7], refs[-7], refs[-6:-2], refs[-2:]

    @pl.when(pl.program_id(0) == 0)
    def _():
        pre = sum_cores(half_ref, other_ref)
        parts = [gate * sig * up for gate, up, sig in gates(pre, pre.shape[1] // 4)]
        hidden_ref[...] = jnp.concatenate(parts, axis=1).astype(BF)

    spread_back(hidden_ref, fetch(weights, lo, hi, buf, sem), outs)


def backward_kernel(lo, hi, half_ref, other_ref, ghalf_ref, gother_ref, *refs):
    weights, grad_ref, outs, (buf, sem) = refs[:-7], refs[-7], refs[-6:-2], refs[-2:]

    @pl.when(pl.program_id(0) == 0)
    def _():
        pre = sum_cores(half_ref, other_ref)
        hid = pre.shape[1] // 4
        grad_hidden = sum_cores(ghalf_ref, gother_ref)
        parts = []
        for s, (gate, up, sig) in enumerate(gates(pre, hid)):
            grad = grad_hidden[:, s * hid : (s + 1) * hid]
            parts += [grad * up * sig * (1.0 + gate * (1.0 - sig)), grad * (gate * sig)]
        grad_ref[...] = jnp.concatenate(parts, axis=1).astype(BF)

    spread_back(grad_ref, fetch(weights, lo, hi, buf, sem), outs)


def middle(kernel, name, halves, weights, lo, hi):
    count = halves[0].shape[0]
    seg = weights[0].shape[0]
    chunk = count // N_Y
    cols = 2 * (hi - lo)
    first, *pieces = pl.pallas_call(
        functools.partial(kernel, lo, hi),
        grid=(N_X,),
        in_specs=[whole(h.shape) for h in halves] + [ANY] * len(weights),
        out_specs=[whole((count, cols))] + row_specs(N_Y, chunk, seg),
        out_shape=[like(count, cols)] + [like(chunk, N_X * seg)] * N_Y,
        scratch_shapes=fetch_scratch(weights, lo, hi),
        compiler_params=params(24),
        cost_estimate=cost(COST),
        name=name,
    )(*halves, *weights)
    return first, pieces


def weight_grad_kernel(hidden_ref, grad_ref, *refs):
    tok, cot, outs = refs[:N_Y], refs[N_Y : 2 * N_Y], refs[2 * N_Y : -2]
    buf, sem = refs[-2:]
    k = pl.program_id(0)
    hid = hidden_ref.shape[1] // 2
    dims = (((0,), (0,)), ((), ()))
    gate_up = lax.dot_general(stacked(tok), grad_ref[...], dims, preferred_element_type=F32)
    down = lax.dot_general(stacked(cot), hidden_ref[...], dims, preferred_element_type=F32)
    for s in range(2):
        buf[2 * k + s, :, : 2 * hid] = gate_up[:, 2 * s * hid : (2 * s + 2) * hid].astype(BF)
        buf[2 * k + s, :, 2 * hid :] = down[:, s * hid : (s + 1) * hid].astype(BF)
    for j in range(N_X):

        @pl.when(k == j)
        def _(j=j):
            for i in (2 * j, 2 * j + 1):
                pltpu.make_async_copy(buf.at[i], outs[i], sem.at[i]).start()

    @pl.when(k == N_X - 1)
    def _():
        for i, out in enumerate(outs):
            pltpu.make_async_copy(buf.at[i], out, sem.at[i]).wait()


def weight_grad(hidden, grad_pre, tok_rows, cot_rows):
    hid = hidden.shape[1] // 2
    chunk, width = tok_rows[0].shape
    seg = width // N_X
    count = 2 * N_X
    return pl.pallas_call(
        weight_grad_kernel,
        grid=(N_X,),
        in_specs=[whole(hidden.shape), whole(grad_pre.shape)]
        + row_specs(2 * N_Y, chunk, seg),
        out_specs=[ANY] * count,
        out_shape=[like(seg, 3 * hid)] * count,
        scratch_shapes=[
            pltpu.VMEM((count, seg, 3 * hid), BF),
            pltpu.SemaphoreType.DMA((count,)),
        ],
        compiler_params=params(32),
        cost_estimate=cost(COST),
        name="weight_grad",
    )(hidden, grad_pre, *tok_rows, *cot_rows)


def split_kernel(c_ref, keep_in, give_in, keep_ref, give_ref):
    del c_ref
    keep_ref[...] = keep_in[0].astype(BF)
    give_ref[...] = give_in[0].astype(BF)


def split_master(c, master):
    _, quarter, cols = master.shape
    seg = quarter // N_C
    out = like(seg, cols)
    return pl.pallas_call(
        split_kernel,
        grid_spec=pltpu.PrefetchScalarGridSpec(
            num_scalar_prefetch=1,
            grid=(1,),
            in_specs=[
                pl.BlockSpec((1, seg, cols), lambda i, c: (0, c[0], 0)),
                pl.BlockSpec((1, seg, cols), lambda i, c: (0, 1 - c[0], 0)),
            ],
            out_specs=[pl.BlockSpec((seg, cols), lambda i, c: (0, 0))] * 2,
        ),
        out_shape=[out, out],
        compiler_params=params(16),
        cost_estimate=cost(COST),
        name="split_master",
    )(c, master, master)


def update_kernel(c_ref, master_ref, sums_ref, other_ref, *refs):
    *parts, new_ref, out_ref, grad_ref = refs
    here = pl.program_id(0) == c_ref[0]

    @pl.when(here)
    def _():
        grad_ref[...] = sum(p[...].astype(F32) for p in parts).astype(BF).astype(F32)

    @pl.when(jnp.logical_not(here))
    def _():
        grad_ref[...] = other_ref[...].astype(F32)

    seg, cols = grad_ref.shape
    hid = cols // 3
    ones = jnp.ones((8, hid), F32)
    means = []
    for g in range(3):
        grad = grad_ref[:, g * hid : (g + 1) * hid]
        total = lax.dot_general(
            ones,
            grad * grad,
            (((1,), (1,)), ((), ())),
            precision=lax.Precision.HIGHEST,
            preferred_element_type=F32,
        )
        means.append(total[:1] / hid)
    sums = sums_ref[0] + jnp.concatenate(means, axis=0)
    out_ref[0] = sums
    scale = LEARN_RATE / (jnp.sqrt(sums) + EPSILON)
    tall = jnp.concatenate([scale, jnp.zeros((125, seg), F32)], axis=0).T
    for g in range(3):
        span = pl.ds(g * hid, hid)
        new_ref[:, span] = (master_ref[0, :, span] - grad_ref[:, span] * tall[:, g : g + 1]).astype(BF)


def update(c, master, sums, other, *parts):
    _, quarter, cols = master.shape
    seg = quarter // N_C
    piece = pl.BlockSpec((seg, cols), lambda h, c: (0, 0))
    rows = pl.BlockSpec((seg, cols), lambda h, c: (h, 0))
    lanes = pl.BlockSpec((1, 3, seg), lambda h, c: (0, 0, h))
    return pl.pallas_call(
        update_kernel,
        grid_spec=pltpu.PrefetchScalarGridSpec(
            num_scalar_prefetch=1,
            grid=(N_C,),
            in_specs=[pl.BlockSpec((1, seg, cols), lambda h, c: (0, h, 0)), lanes]
            + [piece] * (1 + len(parts)),
            out_specs=[rows, lanes],
            scratch_shapes=[pltpu.VMEM((seg, cols), F32)],
        ),
        out_shape=[like(quarter, cols), like(*sums.shape, dtype=F32)],
        compiler_params=params(24),
        cost_estimate=cost(COST),
        name="update_master",
    )(c, master, sums, other, *parts)


def exchange(blocks):
    return lax.all_to_all(blocks, ("z", "c"), split_axis=0, concat_axis=0, tiled=True)


def after(value, *firsts):
    return lax.optimization_barrier((value, *firsts))[0]


def local(tokens, cotangent, route_ids, router_weights, master, accumulator):
    hid = master.shape[2] // 3
    x = lax.axis_index("x").reshape(1)
    core = lax.axis_index("c").reshape(1)
    merge = lambda a: a.reshape((N_Z * N_C,) + a.shape[2:])

    own, give = split_master(core, master)
    got = swap_core(give)
    own_weights = ring_gather(own, "x", 1)
    got_weights = ring_gather(got, "x", -1)
    weights = [w for pair in zip(own_weights, got_weights) for w in pair]

    tok_send, out_tab, in_tab = select(
        x, after(route_ids, own), router_weights, tokens, False, True
    )
    tok_packed = exchange(merge(tok_send))
    (cot_send,) = select(x, route_ids, router_weights, after(cotangent, tok_send), True, False)
    cot_packed = exchange(merge(cot_send))

    tok_packed = after(tok_packed, own_weights[1], own_weights[3])
    tok_rows = ring_gather(unpack(tok_packed), "y", 1)
    cot_packed = after(cot_packed, tok_rows[1], tok_rows[3], got_weights[1], got_weights[3])
    cot_rows = ring_gather(unpack(cot_packed), "y", -1)

    pre = project(tok_rows, weights, 0, 2 * hid)
    pre_other = swap_core(pre)
    hidden, out_pieces = middle(
        forward_kernel, "forward_rows", (pre, pre_other), weights, 2 * hid, 3 * hid
    )
    grad_hidden = project(cot_rows, weights, 2 * hid, 3 * hid)
    grad_other = after(swap_core(grad_hidden), hidden)
    grad_pre, in_pieces = middle(
        backward_kernel,
        "backward_rows",
        (pre, pre_other, grad_hidden, grad_other),
        weights,
        0,
        2 * hid,
    )
    grads = weight_grad(hidden, grad_pre, tok_rows, cot_rows)

    out_parts = ring_scatter(out_pieces, "y", 1)
    in_parts = ring_scatter(in_pieces, "y", -1)
    own_parts = ring_scatter(grads[::2], "x", 1)
    got_parts = ring_scatter(grads[1::2], "x", -1)

    output = combine(x, out_tab, exchange(pack(*out_parts)))
    input_grad = combine(x, in_tab, exchange(pack(*in_parts)))

    got_grad = sum(p.astype(F32) for p in got_parts).astype(BF)
    new, sums = update(core, master, accumulator, swap_core(got_grad), *own_parts)
    return output, input_grad, swap_core(new)[None], sums


def solution(mesh):
    fine = Mesh(mesh.devices.reshape(N_X, N_Z, N_Y, N_C), ("x", "z", "y", "c"))
    rows = P(("x", "z", "y", "c"), None)
    weights = P(("z", "y", "c"), "x", None)
    sums = P(("z", "y", "c"), None, "x")
    return jax.shard_map(
        local,
        mesh=fine,
        in_specs=(rows, rows, rows, rows, weights, sums),
        out_specs=(rows, rows, weights, sums),
        check_vma=False,
    )
```

```python
import functools

import jax
import jax.numpy as jnp
from jax import lax
from jax.experimental import pallas as pl
from jax.experimental.pallas import tpu as pltpu
from jax.sharding import Mesh, PartitionSpec as P


N_X, N_Z, N_Y, N_C = 4, 8, 4, 2
CAP = 5
LEARN_RATE = 0.01
EPSILON = 1e-06
BF = jnp.bfloat16
F32 = jnp.float32
COST = 100
ROOM = 60
SHARE = 28
BLK = 256


def swap_core(a):
    return lax.ppermute(a, "c", [(0, 1), (1, 0)])


def swap(a, axis, bits):
    return lax.ppermute(a, axis, [(i, i ^ bits) for i in range(lax.axis_size(axis))])


def shift(a, axis, step):
    n = lax.axis_size(axis)
    return lax.ppermute(a, axis, [(i, (i + step) % n) for i in range(n)])


def after(value, *firsts):
    return lax.optimization_barrier((value, *firsts))[0]


def iota(shape, dim):
    return lax.broadcasted_iota(jnp.int32, shape, dim)


def params(mib, **kw):
    return pltpu.CompilerParams(vmem_limit_bytes=mib << 20, **kw)


def like(*shape, dtype=BF):
    return jax.ShapeDtypeStruct(shape, dtype)


def dot_nn(a, b):
    return jnp.dot(a, b, preferred_element_type=F32)


def dot_nt(a, b):
    return lax.dot_general(a, b, (((1,), (1,)), ((), ())), preferred_element_type=F32)


def dot_tn(a, b):
    return lax.dot_general(a, b, (((0,), (0,)), ((), ())), preferred_element_type=F32)


def cost(micros):
    return pl.CostEstimate(
        flops=micros * 10**9, bytes_accessed=micros * 10**6, transcendentals=0
    )


def select_kernel(scaled, with_tab, x_ref, ids_ref, w_ref, *refs):
    del x_ref
    segs, refs = refs[:N_X], refs[N_X:]
    send_ref, refs = refs[0], refs[1:]
    if with_tab:
        (out_tab, in_tab), refs = refs[:2], refs[2:]
    sel_ref, row_ref = refs
    tok = ids_ref.shape[0]
    packed = send_ref.shape[2]
    blocks = packed // CAP

    @pl.when(pl.program_id(0) == 0)
    def _():
        lane = iota((tok, 128), 1)
        named = jnp.zeros((tok, 128), F32)
        weight = jnp.zeros((tok, 128), F32)
        for k in range(ids_ref.shape[1]):
            hit = ids_ref[:, k : k + 1] == lane
            named = jnp.where(hit, 1.0, named)
            weight = jnp.where(hit, w_ref[:, k : k + 1], weight)
        earlier = jnp.where(iota((tok, tok), 1) < iota((tok, tok), 0), 1.0, 0.0).astype(BF)
        place = dot_nn(earlier, named.astype(BF))
        code = jnp.where(named > 0, place + 1.0, 0.0)
        code_t = code.T
        weight_t = weight.T
        r = iota((packed, 1), 0)
        slot = (r % CAP + 1).astype(F32)
        shape = (packed, blocks * tok)
        diag = iota(shape, 0) // CAP == iota(shape, 1) // tok
        for e in range(N_Z):
            block = pl.ds(e * packed, packed)
            picked = jnp.broadcast_to(code_t[e : e + 1, :], (packed, tok)) == slot
            ones = jnp.where(picked, 1.0, 0.0)
            wide = jnp.concatenate([ones] * blocks, axis=1)
            sel_ref[block, :] = jnp.where(diag, wide, 0.0).astype(BF)
            if scaled:
                part = jnp.where(picked, jnp.broadcast_to(weight_t[e : e + 1, :], (packed, tok)), 0.0)
                row_ref[block, :] = jnp.broadcast_to(jnp.sum(part, axis=1, keepdims=True), (packed, 128))
        if with_tab:
            total = N_Z * packed
            l = iota((128, total), 1)
            spread = jnp.where(l // packed == iota((128, total), 0), 1.0, 0.0).astype(BF)
            l = iota((tok, total), 1) % packed
            valid = (dot_nn(code.astype(BF), spread) == (l % CAP + 1).astype(F32)) & (l < blocks * CAP)
            in_tab[...] = jnp.where(valid, 1.0, 0.0).astype(BF)
            out_tab[...] = jnp.where(valid, dot_nn(weight.astype(BF), spread), 0.0).astype(BF)

    wide = jnp.concatenate([s[...] for s in segs], axis=1)
    stack = jnp.concatenate([wide[:, q * BLK : (q + 1) * BLK] for q in range(blocks)], axis=0)
    rows = dot_nn(sel_ref[...], stack)
    if scaled:
        rows = rows * row_ref[:, :1]
    send_ref[...] = rows.astype(BF).reshape(send_ref.shape)


def packed_rows(width):
    blocks = width // N_C // BLK
    return -(-blocks * CAP // 8) * 8


def select(x, ids, weights, data, scaled, with_tab):
    tok, width = data.shape
    seg = width // (N_X * N_C)
    packed = packed_rows(width)
    blocks = packed // CAP
    total = N_Z * packed
    seg_spec = lambda k: pl.BlockSpec(
        (tok, seg), lambda c, x: (0, lax.bitwise_xor(x[0], k) * N_C + c)
    )
    out_specs = [pl.BlockSpec((N_Z, 1, packed, BLK), lambda c, x: (0, c, 0, 0))]
    out_shape = [like(N_Z, N_C, packed, BLK)]
    if with_tab:
        out_specs += [pl.BlockSpec((tok, total), lambda c, x: (0, 0))] * 2
        out_shape += [like(tok, total)] * 2
    return pl.pallas_call(
        functools.partial(select_kernel, scaled, with_tab),
        grid_spec=pltpu.PrefetchScalarGridSpec(
            num_scalar_prefetch=1,
            grid=(N_C,),
            in_specs=[
                pl.BlockSpec(ids.shape, lambda c, x: (0, 0)),
                pl.BlockSpec(weights.shape, lambda c, x: (0, 0)),
            ]
            + [seg_spec(k) for k in range(N_X)],
            out_specs=out_specs,
            scratch_shapes=[
                pltpu.VMEM((total, blocks * tok), BF),
                pltpu.VMEM((total, 128), F32),
            ],
        ),
        out_shape=out_shape,
        compiler_params=params(SHARE),
        cost_estimate=cost(COST),
        name="select_cot" if scaled else "select_tok",
    )(x, ids, weights, *([data] * N_X))


GROWS = N_Z * CAP


def unpack_kernel(in_ref, out_ref):
    packed = in_ref.shape[1]
    blocks = packed // CAP
    shape = (blocks * GROWS, N_Z * packed)
    row, col = iota(shape, 0), iota(shape, 1)
    place = row % GROWS
    want = place // CAP * packed + row // GROWS * CAP + place % CAP
    perm = jnp.where(col == want, 1.0, 0.0).astype(BF)
    out = dot_nn(perm, in_ref[...].reshape(N_Z * packed, BLK))
    for q in range(blocks):
        out_ref[:, pl.ds(q * BLK, BLK)] = out[q * GROWS : (q + 1) * GROWS].astype(BF)


def unpack(packed):
    srcs, rows, _ = packed.shape
    width = rows // CAP * BLK
    return pl.pallas_call(
        unpack_kernel,
        grid=(srcs // N_Z,),
        in_specs=[pl.BlockSpec((N_Z, rows, BLK), lambda h: (h, 0, 0))],
        out_specs=pl.BlockSpec((GROWS, width), lambda h: (h, 0)),
        out_shape=like(srcs * CAP, width),
        compiler_params=params(SHARE),
        cost_estimate=cost(COST),
        name="unpack_rows",
    )(packed)


def pack_kernel(*refs):
    *parts, send_ref = refs
    packed = send_ref.shape[1]
    blocks = packed // CAP
    total = sum(r[...].astype(F32) for r in parts)
    stack = jnp.concatenate(
        [total[:, q * BLK : (q + 1) * BLK] for q in range(blocks)], axis=0
    ).astype(BF)
    shape = (N_Z * packed, blocks * GROWS)
    row, col = iota(shape, 0), iota(shape, 1)
    r = row % packed
    want = r // CAP * GROWS + row // packed * CAP + r % CAP
    perm = jnp.where((col == want) & (r < blocks * CAP), 1.0, 0.0).astype(BF)
    send_ref[...] = dot_nn(perm, stack).astype(BF).reshape(send_ref.shape)


def pack(*parts):
    rows, width = parts[0].shape
    packed = packed_rows(width * N_C)
    return pl.pallas_call(
        pack_kernel,
        grid=(rows // GROWS,),
        in_specs=[pl.BlockSpec((GROWS, width), lambda h: (h, 0))] * len(parts),
        out_specs=pl.BlockSpec((N_Z, packed, BLK), lambda h: (h, 0, 0)),
        out_shape=like(rows // CAP, packed, BLK),
        compiler_params=params(SHARE),
        cost_estimate=cost(COST),
        name="pack_rows",
    )(*parts)


GROUP = 7


def combine_kernel(x_ref, tab_ref, back_ref, out_ref, big_ref, acc_ref):
    del x_ref
    c, k = pl.program_id(0), pl.program_id(1)
    tok, total = tab_ref.shape
    packed = back_ref.shape[2]
    blocks = packed // CAP
    seg = out_ref.shape[1]

    @pl.when((c == 0) & (k == 0))
    def _():
        where = iota((tok, total), 1) % packed // CAP
        for q in range(blocks):
            big_ref[pl.ds(q * tok, tok), :] = jnp.where(where == q, tab_ref[...], jnp.zeros((), BF))

    @pl.when(k == 0)
    def _():
        back = back_ref[...].reshape(total, BLK)

        def block(i, carry):
            span = pl.ds(pl.multiple_of(i * GROUP * tok, tok), GROUP * tok)
            out = dot_nn(big_ref[span, :], back).astype(BF)
            for q in range(GROUP):
                cols = pl.ds(pl.multiple_of((i * GROUP + q) * BLK, BLK), BLK)
                acc_ref[:, cols] = out[q * tok : (q + 1) * tok]
            return carry

        lax.fori_loop(0, blocks // GROUP, block, 0)

    for j in range(N_X):

        @pl.when(k == j)
        def _(j=j):
            out_ref[...] = acc_ref[:, pl.ds(j * seg, seg)]


def combine(x, tab, back):
    tok, total = tab.shape
    _, packed, _ = back.shape
    width = packed // CAP * BLK * N_C
    seg = width // (N_X * N_C)
    return pl.pallas_call(
        combine_kernel,
        grid_spec=pltpu.PrefetchScalarGridSpec(
            num_scalar_prefetch=1,
            grid=(N_C, N_X),
            in_specs=[
                pl.BlockSpec((tok, total), lambda c, k, x: (0, 0)),
                pl.BlockSpec((N_Z, 1, packed, BLK), lambda c, k, x: (0, c, 0, 0)),
            ],
            out_specs=pl.BlockSpec(
                (tok, seg), lambda c, k, x: (0, lax.bitwise_xor(x[0], k) * N_C + c)
            ),
            scratch_shapes=[
                pltpu.VMEM((packed // CAP * tok, total), BF),
                pltpu.VMEM((tok, width // N_C), BF),
            ],
        ),
        out_shape=like(tok, width),
        compiler_params=params(SHARE),
        cost_estimate=cost(COST),
        name="combine_rows",
    )(x, tab, back.reshape(N_Z, N_C, packed, BLK))


def gather_x(piece, near):
    far_side = near ^ 2
    got = {near: swap(piece, "x", near), far_side: swap(piece, "x", far_side)}
    return [piece, got[1], swap(got[far_side], "x", near), got[3]]


def scatter_x(here, pair, other, near):
    moved = swap(pair, "x", near)
    joint = (other.astype(F32) + moved[1].astype(F32)).astype(BF)
    return here, moved, swap(joint, "x", near ^ 2)


def gather_y(rows, step):
    ahead, behind = shift(rows, "y", -1), shift(rows, "y", 1)
    far = shift(behind if step == 1 else ahead, "y", step)
    return [rows, ahead, far, behind]


def scatter_y(pieces):
    return [pieces[0]] + [shift(pieces[k], "y", k) for k in (2, 1, 3)]


ANY = pl.BlockSpec(memory_space=pl.ANY)


def stacked(rows):
    return jnp.concatenate([r[...] for r in rows], axis=0)


def fetch(weights, lo, hi, buf, sem):
    k = pl.program_id(0)

    @pl.when(k == 0)
    def _():
        for j, w in enumerate(weights):
            pltpu.make_async_copy(
                w.at[:, pl.ds(lo, hi - lo)], buf.at[j], sem.at[j]
            ).start()

    for s in range(2):
        j = 2 * k + s
        pltpu.make_async_copy(
            weights[0].at[:, pl.ds(lo, hi - lo)], buf.at[j], sem.at[j]
        ).wait()
    return jnp.concatenate([buf[2 * k], buf[2 * k + 1]], axis=1)


def fetch_scratch(weights, lo, hi):
    count = len(weights)
    return [
        pltpu.VMEM((count, weights[0].shape[0], hi - lo), BF),
        pltpu.SemaphoreType.DMA((count,)),
    ]


def row_specs(count, chunk, seg):
    return [pl.BlockSpec((chunk, seg), lambda k: (0, k))] * count


def whole(shape):
    return pl.BlockSpec(shape, lambda k: (0,) * len(shape))


def project_kernel(lo, hi, *refs):
    rows, weights, (out_ref, buf, sem) = refs[:N_Y], refs[N_Y:-3], refs[-3:]
    part = dot_nn(stacked(rows), fetch(weights, lo, hi, buf, sem))

    @pl.when(pl.program_id(0) == 0)
    def _():
        out_ref[...] = part

    @pl.when(pl.program_id(0) > 0)
    def _():
        out_ref[...] += part


def project(rows, weights, lo, hi):
    chunk = rows[0].shape[0]
    seg = weights[0].shape[0]
    shape = (chunk * N_Y, 2 * (hi - lo))
    return pl.pallas_call(
        functools.partial(project_kernel, lo, hi),
        grid=(N_X,),
        in_specs=row_specs(N_Y, chunk, seg) + [ANY] * len(weights),
        out_specs=whole(shape),
        out_shape=like(*shape, dtype=F32),
        scratch_shapes=fetch_scratch(weights, lo, hi),
        compiler_params=params(SHARE),
        cost_estimate=cost(COST),
        name="project_rows",
    )(*rows, *weights)


def sum_cores(half, other):
    mid = half.shape[1] // 2
    return half[...] + jnp.concatenate([other[:, mid:], other[:, :mid]], axis=1)


def gates(pre, hid):
    for s in range(2):
        gate = pre[:, 2 * s * hid : (2 * s + 1) * hid]
        yield gate, pre[:, (2 * s + 1) * hid : (2 * s + 2) * hid], jax.nn.sigmoid(gate)


def spread_back(value_ref, weights, outs):
    part = lax.dot_general(
        value_ref[...], weights, (((1,), (1,)), ((), ())), preferred_element_type=F32
    ).astype(BF)
    chunk = part.shape[0] // N_Y
    for i, ref in enumerate(outs):
        ref[...] = part[i * chunk : (i + 1) * chunk]


def forward_kernel(lo, hi, half_ref, other_ref, *refs):
    weights, hidden_ref, outs, (buf, sem) = refs[:-7], refs[-7], refs[-6:-2], refs[-2:]

    @pl.when(pl.program_id(0) == 0)
    def _():
        pre = sum_cores(half_ref, other_ref)
        parts = [gate * sig * up for gate, up, sig in gates(pre, pre.shape[1] // 4)]
        hidden_ref[...] = jnp.concatenate(parts, axis=1).astype(BF)

    spread_back(hidden_ref, fetch(weights, lo, hi, buf, sem), outs)


def backward_kernel(lo, hi, half_ref, other_ref, ghalf_ref, gother_ref, *refs):
    weights, grad_ref, outs, (buf, sem) = refs[:-7], refs[-7], refs[-6:-2], refs[-2:]

    @pl.when(pl.program_id(0) == 0)
    def _():
        pre = sum_cores(half_ref, other_ref)
        hid = pre.shape[1] // 4
        grad_hidden = sum_cores(ghalf_ref, gother_ref)
        parts = []
        for s, (gate, up, sig) in enumerate(gates(pre, hid)):
            grad = grad_hidden[:, s * hid : (s + 1) * hid]
            parts += [grad * up * sig * (1.0 + gate * (1.0 - sig)), grad * (gate * sig)]
        grad_ref[...] = jnp.concatenate(parts, axis=1).astype(BF)

    spread_back(grad_ref, fetch(weights, lo, hi, buf, sem), outs)


def middle(kernel, name, halves, weights, lo, hi):
    count = halves[0].shape[0]
    seg = weights[0].shape[0]
    chunk = count // N_Y
    cols = 2 * (hi - lo)
    first, *pieces = pl.pallas_call(
        functools.partial(kernel, lo, hi),
        grid=(N_X,),
        in_specs=[whole(h.shape) for h in halves] + [ANY] * len(weights),
        out_specs=[whole((count, cols))]
        + row_specs(N_Y, chunk, seg),
        out_shape=[like(count, cols)] + [like(chunk, N_X * seg)] * N_Y,
        scratch_shapes=fetch_scratch(weights, lo, hi),
        compiler_params=params(SHARE),
        cost_estimate=cost(COST),
        name=name,
    )(*halves, *weights)
    return first, pieces


def weight_grad_kernel(hidden_ref, grad_ref, *refs):
    tok, cot, outs = refs[:N_Y], refs[N_Y : 2 * N_Y], refs[2 * N_Y : -2]
    buf, sem = refs[-2:]
    k = pl.program_id(0)
    hid = hidden_ref.shape[1] // 2
    dims = (((0,), (0,)), ((), ()))
    gate_up = lax.dot_general(stacked(tok), grad_ref[...], dims, preferred_element_type=F32)
    down = lax.dot_general(stacked(cot), hidden_ref[...], dims, preferred_element_type=F32)
    for s in range(2):
        buf[2 * k + s, :, : 2 * hid] = gate_up[:, 2 * s * hid : (2 * s + 2) * hid].astype(BF)
        buf[2 * k + s, :, 2 * hid :] = down[:, s * hid : (s + 1) * hid].astype(BF)
    def copies(j):
        for i, near in enumerate((1, 3)):
            here, pair, other = outs[3 * i : 3 * i + 3]
            dst = {0: here, near: pair.at[0], 2: pair.at[1], near ^ 2: other}[j]
            yield pltpu.make_async_copy(buf.at[2 * j + i], dst, sem.at[2 * j + i])

    for j in range(N_X):

        @pl.when(k == j)
        def _(j=j):
            for c in copies(j):
                c.start()

    @pl.when(k == N_X - 1)
    def _():
        for j in range(N_X):
            for c in copies(j):
                c.wait()


def weight_grad(hidden, grad_pre, tok_rows, cot_rows):
    hid = hidden.shape[1] // 2
    chunk, width = tok_rows[0].shape
    seg = width // N_X
    one, two = like(seg, 3 * hid), like(2, seg, 3 * hid)
    outs = [one, two, one, one, two, one]
    return pl.pallas_call(
        weight_grad_kernel,
        grid=(N_X,),
        in_specs=[whole(hidden.shape), whole(grad_pre.shape)]
        + row_specs(2 * N_Y, chunk, seg),
        out_specs=[ANY] * len(outs),
        out_shape=outs,
        scratch_shapes=[
            pltpu.VMEM((2 * N_X, seg, 3 * hid), BF),
            pltpu.SemaphoreType.DMA((2 * N_X,)),
        ],
        compiler_params=params(SHARE),
        cost_estimate=cost(COST),
        name="weight_grad",
    )(hidden, grad_pre, *tok_rows, *cot_rows)


def split_kernel(c_ref, keep_in, give_in, keep_ref, give_ref):
    del c_ref
    keep_ref[...] = keep_in[0].astype(BF)
    give_ref[...] = give_in[0].astype(BF)


def split_master(c, master):
    _, quarter, cols = master.shape
    seg = quarter // N_C
    out = like(seg, cols)
    return pl.pallas_call(
        split_kernel,
        grid_spec=pltpu.PrefetchScalarGridSpec(
            num_scalar_prefetch=1,
            grid=(1,),
            in_specs=[
                pl.BlockSpec((1, seg, cols), lambda i, c: (0, c[0], 0)),
                pl.BlockSpec((1, seg, cols), lambda i, c: (0, 1 - c[0], 0)),
            ],
            out_specs=[pl.BlockSpec((seg, cols), lambda i, c: (0, 0))] * 2,
        ),
        out_shape=[out, out],
        compiler_params=params(ROOM),
        cost_estimate=cost(COST),
        name="split_master",
    )(c, master, master)


def update_kernel(c_ref, master_ref, sums_ref, other_ref, *refs):
    *parts, new_ref, out_ref, grad_ref = refs
    here = pl.program_id(0) == c_ref[0]

    @pl.when(here)
    def _():
        grad_ref[...] = sum(p[...].astype(F32) for p in parts).astype(BF).astype(F32)

    @pl.when(jnp.logical_not(here))
    def _():
        grad_ref[...] = other_ref[...].astype(F32)

    seg, cols = grad_ref.shape
    hid = cols // 3
    ones = jnp.ones((8, hid), F32)
    means = []
    for g in range(3):
        grad = grad_ref[:, g * hid : (g + 1) * hid]
        total = lax.dot_general(
            ones,
            grad * grad,
            (((1,), (1,)), ((), ())),
            precision=lax.Precision.HIGHEST,
            preferred_element_type=F32,
        )
        means.append(total[:1] / hid)
    sums = sums_ref[0] + jnp.concatenate(means, axis=0)
    out_ref[0] = sums
    scale = LEARN_RATE / (jnp.sqrt(sums) + EPSILON)
    tall = jnp.concatenate([scale, jnp.zeros((125, seg), F32)], axis=0).T
    for g in range(3):
        span = pl.ds(g * hid, hid)
        new_ref[:, span] = (master_ref[0, :, span] - grad_ref[:, span] * tall[:, g : g + 1]).astype(BF)


def update(c, master, sums, other, *parts):
    _, quarter, cols = master.shape
    seg = quarter // N_C
    piece = pl.BlockSpec((seg, cols), lambda h, c: (0, 0))
    first = pl.BlockSpec((pl.squeezed, seg, cols), lambda h, c: (0, 0, 0))
    rows = pl.BlockSpec((seg, cols), lambda h, c: (h, 0))
    lanes = pl.BlockSpec((1, 3, seg), lambda h, c: (0, 0, h))
    return pl.pallas_call(
        update_kernel,
        grid_spec=pltpu.PrefetchScalarGridSpec(
            num_scalar_prefetch=1,
            grid=(N_C,),
            in_specs=[pl.BlockSpec((1, seg, cols), lambda h, c: (0, h, 0)), lanes]
            + [piece, piece, first, piece],
            out_specs=[rows, lanes],
            scratch_shapes=[pltpu.VMEM((seg, cols), F32)],
        ),
        out_shape=[like(quarter, cols), like(*sums.shape, dtype=F32)],
        compiler_params=params(SHARE),
        cost_estimate=cost(COST),
        name="update_master",
    )(c, master, sums, other, *parts)


def copy_kernel(in_ref, out_ref):
    out_ref[0] = in_ref[...]


def placed(rows):
    count, cols = rows.shape
    return pl.pallas_call(
        copy_kernel,
        grid=(2,),
        in_specs=[pl.BlockSpec((count // 2, cols), lambda i: (i, 0))],
        out_specs=pl.BlockSpec((1, count // 2, cols), lambda i: (0, i, 0)),
        out_shape=like(1, count, cols),
        compiler_params=params(SHARE),
        cost_estimate=cost(COST),
        name="place_weights",
    )(rows)


def exchange(blocks):
    return lax.all_to_all(blocks, ("z", "c"), split_axis=0, concat_axis=0, tiled=True)


def local(tokens, cotangent, route_ids, router_weights, master, accumulator):
    hid = master.shape[2] // 3
    x = lax.axis_index("x").reshape(1)
    core = lax.axis_index("c").reshape(1)
    merge = lambda a: a.reshape((N_Z * N_C,) + a.shape[2:])

    tok_send, out_tab, in_tab = select(x, route_ids, router_weights, tokens, False, True)
    tok_packed = exchange(merge(tok_send))
    (cot_send,) = select(x, route_ids, router_weights, after(cotangent, tok_send), True, False)
    cot_packed = exchange(merge(cot_send))

    own, give = split_master(core, master)
    got = swap_core(give)
    own_weights = gather_x(own, 1)
    got_weights = gather_x(got, 3)
    weights = [w for pair in zip(own_weights, got_weights) for w in pair]

    tok_packed = after(tok_packed, own_weights[1], own_weights[3])
    tok_rows = gather_y(unpack(tok_packed), 1)
    cot_packed = after(cot_packed, tok_rows[1], tok_rows[3], got_weights[1], got_weights[3])
    cot_rows = gather_y(unpack(cot_packed), -1)

    pre = project(tok_rows, weights, 0, 2 * hid)
    pre_other = swap_core(pre)
    hidden, out_pieces = middle(
        forward_kernel, "forward_rows", (pre, pre_other), weights, 2 * hid, 3 * hid
    )
    grad_hidden = project(cot_rows, weights, 2 * hid, 3 * hid)
    grad_other = after(swap_core(grad_hidden), hidden)
    grad_pre, in_pieces = middle(
        backward_kernel,
        "backward_rows",
        (pre, pre_other, grad_hidden, grad_other),
        weights,
        0,
        2 * hid,
    )
    grads = weight_grad(hidden, grad_pre, tok_rows, cot_rows)

    out_parts = scatter_y(out_pieces)
    in_pieces = [after(p, *grads[1::3]) for p in in_pieces]
    in_parts = scatter_y(in_pieces)
    own_parts = scatter_x(*grads[:3], 1)
    here, moved, joint = scatter_x(*grads[3:], 3)

    out_back = exchange(pack(*out_parts))
    in_back = exchange(pack(*in_parts))

    output = combine(x, out_tab, out_back)
    joint = after(joint, out_back)
    got_grad = sum(p.astype(F32) for p in (here, moved[0], joint)).astype(BF)
    new, sums = update(core, master, accumulator, swap_core(got_grad), *own_parts)
    new_weights = placed(swap_core(new))

    input_grad = combine(x, in_tab, in_back)
    return output, input_grad, new_weights, sums


def solution(mesh):
    fine = Mesh(mesh.devices.reshape(N_X, N_Z, N_Y, N_C), ("x", "z", "y", "c"))
    rows = P(("x", "z", "y", "c"), None)
    weights = P(("z", "y", "c"), "x", None)
    sums = P(("z", "y", "c"), None, "x")
    return jax.shard_map(
        local,
        mesh=fine,
        in_specs=(rows, rows, rows, rows, weights, sums),
        out_specs=(rows, rows, weights, sums),
        check_vma=False,
    )
```

```python
import functools

import jax
import jax.numpy as jnp
from jax import lax
from jax.experimental import pallas as pl
from jax.experimental.pallas import tpu as pltpu
from jax.sharding import Mesh, PartitionSpec as P


N_X, N_Z, N_Y, N_C = 4, 8, 4, 2
CAP = 5
LEARN_RATE = 0.01
EPSILON = 1e-06
BF = jnp.bfloat16
F32 = jnp.float32
COST = 100
ROOM = 60
SHARE = 28
BLK = 256


def swap_core(a):
    return lax.ppermute(a, "c", [(0, 1), (1, 0)])


def swap(a, axis, bits):
    return lax.ppermute(a, axis, [(i, i ^ bits) for i in range(lax.axis_size(axis))])


def shift(a, axis, step):
    n = lax.axis_size(axis)
    return lax.ppermute(a, axis, [(i, (i + step) % n) for i in range(n)])


def after(value, *firsts):
    return lax.optimization_barrier((value, *firsts))[0]


def iota(shape, dim):
    return lax.broadcasted_iota(jnp.int32, shape, dim)


def params(mib, **kw):
    return pltpu.CompilerParams(vmem_limit_bytes=mib << 20, **kw)


def like(*shape, dtype=BF):
    return jax.ShapeDtypeStruct(shape, dtype)


def dot_nn(a, b):
    return jnp.dot(a, b, preferred_element_type=F32)


def dot_nt(a, b):
    return lax.dot_general(a, b, (((1,), (1,)), ((), ())), preferred_element_type=F32)


def dot_tn(a, b):
    return lax.dot_general(a, b, (((0,), (0,)), ((), ())), preferred_element_type=F32)


def cost(micros):
    return pl.CostEstimate(
        flops=micros * 10**9, bytes_accessed=micros * 10**6, transcendentals=0
    )


HEAD = 8 * CAP


def table_lanes(packed):
    l = iota((1, N_Z * packed), 1)
    tail = packed - HEAD
    low = l < N_Z * HEAD
    rest = l - N_Z * HEAD
    return jnp.where(low, l // HEAD, rest // tail), jnp.where(low, l % HEAD, HEAD + rest % tail)


def select_kernel(scaled, with_tab, x_ref, ids_ref, w_ref, *refs):
    del x_ref
    segs, refs = refs[:N_X], refs[N_X:]
    send_ref, refs = refs[0], refs[1:]
    if with_tab:
        (out_tab, in_tab), refs = refs[:2], refs[2:]
    sel_ref, row_ref = refs
    tok = ids_ref.shape[1]
    packed = send_ref.shape[2]
    blocks = packed // CAP

    @pl.when(pl.program_id(0) == 0)
    def _():
        expert = iota((128, tok), 0)
        named = jnp.zeros((128, tok), F32)
        weight_t = jnp.zeros((128, tok), F32)
        for k in range(ids_ref.shape[0]):
            hit = ids_ref[k : k + 1, :] == expert
            named = jnp.where(hit, 1.0, named)
            weight_t = jnp.where(hit, w_ref[k : k + 1, :], weight_t)
        earlier = jnp.where(iota((tok, tok), 0) < iota((tok, tok), 1), 1.0, 0.0).astype(BF)
        place = dot_nn(named.astype(BF), earlier)
        code_t = jnp.where(named > 0, place + 1.0, 0.0)
        r = iota((packed, 1), 0)
        slot = (r % CAP + 1).astype(F32)
        diag = r // CAP == iota((1, blocks * tok), 1) // tok
        for e in range(N_Z):
            block = pl.ds(e * packed, packed)
            picked = jnp.broadcast_to(code_t[e : e + 1, :], (packed, tok)) == slot
            ones = jnp.where(picked, 1.0, 0.0)
            wide = jnp.concatenate([ones] * blocks, axis=1)
            sel_ref[block, :] = jnp.where(diag, wide, 0.0).astype(BF)
            if scaled:
                part = jnp.where(picked, jnp.broadcast_to(weight_t[e : e + 1, :], (packed, tok)), 0.0)
                row_ref[block, :] = jnp.broadcast_to(jnp.sum(part, axis=1, keepdims=True), (packed, 128))
        if with_tab:
            total = N_Z * packed
            code, weight = code_t.T.astype(BF), weight_t.T.astype(BF)
            e, r = table_lanes(packed)
            spread = jnp.where(e == iota((128, 1), 0), 1.0, 0.0).astype(BF)
            slot = jnp.where(r < blocks * CAP, (r % CAP + 1).astype(F32), -1.0)
            valid = dot_nn(code, spread) == slot
            in_tab[...] = jnp.where(valid, 1.0, 0.0).astype(BF)
            out_tab[...] = jnp.where(valid, dot_nn(weight, spread), 0.0).astype(BF)

    wide = jnp.concatenate([s[...] for s in segs], axis=1)
    stack = jnp.concatenate([wide[:, q * BLK : (q + 1) * BLK] for q in range(blocks)], axis=0)
    rows = dot_nn(sel_ref[...], stack)
    if scaled:
        rows = rows * row_ref[:, :1]
    send_ref[...] = rows.astype(BF).reshape(send_ref.shape)


def packed_rows(width):
    blocks = width // N_C // BLK
    return -(-blocks * CAP // 8) * 8


def select(x, ids, weights, data, scaled, with_tab):
    tok, width = data.shape
    seg = width // (N_X * N_C)
    packed = packed_rows(width)
    blocks = packed // CAP
    total = N_Z * packed
    seg_spec = lambda k: pl.BlockSpec(
        (tok, seg), lambda c, x: (0, lax.bitwise_xor(x[0], k) * N_C + c)
    )
    out_specs = [pl.BlockSpec((N_Z, 1, packed, BLK), lambda c, x: (0, c, 0, 0))]
    out_shape = [like(N_Z, N_C, packed, BLK)]
    if with_tab:
        out_specs += [pl.BlockSpec((tok, total), lambda c, x: (0, 0))] * 2
        out_shape += [like(tok, total)] * 2
    return pl.pallas_call(
        functools.partial(select_kernel, scaled, with_tab),
        grid_spec=pltpu.PrefetchScalarGridSpec(
            num_scalar_prefetch=1,
            grid=(N_C,),
            in_specs=[
                pl.BlockSpec(ids.shape, lambda c, x: (0, 0)),
                pl.BlockSpec(weights.shape, lambda c, x: (0, 0)),
            ]
            + [seg_spec(k) for k in range(N_X)],
            out_specs=out_specs,
            scratch_shapes=[
                pltpu.VMEM((total, blocks * tok), BF),
                pltpu.VMEM((total, 128), F32),
            ],
        ),
        out_shape=out_shape,
        compiler_params=params(ROOM),
        cost_estimate=cost(COST),
        name="select_cot" if scaled else "select_tok",
    )(x, ids, weights, *([data] * N_X))


GROWS = N_Z * CAP


def unpack_kernel(in_ref, out_ref):
    packed = in_ref.shape[1]
    blocks = packed // CAP
    row, col = iota((blocks * GROWS, 1), 0), iota((1, N_Z * packed), 1)
    place = row % GROWS
    want = place // CAP * packed + row // GROWS * CAP + place % CAP
    perm = jnp.where(col == want, 1.0, 0.0).astype(BF)
    out = dot_nn(perm, in_ref[...].reshape(N_Z * packed, BLK))
    for q in range(blocks):
        out_ref[:, pl.ds(q * BLK, BLK)] = out[q * GROWS : (q + 1) * GROWS].astype(BF)


def unpack(packed):
    srcs, rows, _ = packed.shape
    width = rows // CAP * BLK
    return pl.pallas_call(
        unpack_kernel,
        grid=(srcs // N_Z,),
        in_specs=[pl.BlockSpec((N_Z, rows, BLK), lambda h: (h, 0, 0))],
        out_specs=pl.BlockSpec((GROWS, width), lambda h: (h, 0)),
        out_shape=like(srcs * CAP, width),
        compiler_params=params(SHARE),
        cost_estimate=cost(COST),
        name="unpack_rows",
    )(packed)


def pack_kernel(*refs):
    *parts, send_ref = refs
    packed = send_ref.shape[1]
    blocks = packed // CAP
    total = sum(r[...].astype(F32) for r in parts)
    stack = jnp.concatenate(
        [total[:, q * BLK : (q + 1) * BLK] for q in range(blocks)], axis=0
    ).astype(BF)
    row, col = iota((N_Z * packed, 1), 0), iota((1, blocks * GROWS), 1)
    r = row % packed
    want = r // CAP * GROWS + row // packed * CAP + r % CAP
    perm = jnp.where(col == jnp.where(r < blocks * CAP, want, -1), 1.0, 0.0).astype(BF)
    send_ref[...] = dot_nn(perm, stack).astype(BF).reshape(send_ref.shape)


def pack(*parts):
    rows, width = parts[0].shape
    packed = packed_rows(width * N_C)
    return pl.pallas_call(
        pack_kernel,
        grid=(rows // GROWS,),
        in_specs=[pl.BlockSpec((GROWS, width), lambda h: (h, 0))] * len(parts),
        out_specs=pl.BlockSpec((N_Z, packed, BLK), lambda h: (h, 0, 0)),
        out_shape=like(rows // CAP, packed, BLK),
        compiler_params=params(SHARE),
        cost_estimate=cost(COST),
        name="pack_rows",
    )(*parts)


def combine_kernel(x_ref, tab_ref, back_ref, out_ref, head_ref, tail_ref, acc_ref):
    del x_ref
    c, k = pl.program_id(0), pl.program_id(1)
    tok, total = tab_ref.shape
    packed = back_ref.shape[2]
    seg = out_ref.shape[1]
    heads = HEAD // CAP
    tails = packed // CAP - heads
    cut = N_Z * HEAD

    @pl.when((c == 0) & (k == 0))
    def _():
        block = table_lanes(packed)[1] // CAP
        for q in range(heads):
            here = jnp.where(block[:, :cut] == q, 1.0, 0.0).astype(BF)
            head_ref[pl.ds(q * tok, tok), :] = tab_ref[:, :cut] * here
        for q in range(tails):
            here = jnp.where(block[:, cut:] == heads + q, 1.0, 0.0).astype(BF)
            tail_ref[pl.ds(q * tok, tok), :] = tab_ref[:, cut:] * here

    @pl.when(k == 0)
    def _():
        back = back_ref[:, 0]
        for ref, first, count, rows in (
            (head_ref, 0, heads, back[:, :HEAD]),
            (tail_ref, heads, tails, back[:, HEAD:]),
        ):
            out = dot_nn(ref[...], rows.reshape(ref.shape[1], BLK)).astype(BF)
            for q in range(count):
                acc_ref[:, pl.ds((first + q) * BLK, BLK)] = out[q * tok : (q + 1) * tok]

    for j in range(N_X):

        @pl.when(k == j)
        def _(j=j):
            out_ref[...] = acc_ref[:, pl.ds(j * seg, seg)]


def combine(x, tab, back):
    tok, total = tab.shape
    _, packed, _ = back.shape
    width = packed // CAP * BLK * N_C
    seg = width // (N_X * N_C)
    return pl.pallas_call(
        combine_kernel,
        grid_spec=pltpu.PrefetchScalarGridSpec(
            num_scalar_prefetch=1,
            grid=(N_C, N_X),
            in_specs=[
                pl.BlockSpec((tok, total), lambda c, k, x: (0, 0)),
                pl.BlockSpec((N_Z, 1, packed, BLK), lambda c, k, x: (0, c, 0, 0)),
            ],
            out_specs=pl.BlockSpec(
                (tok, seg), lambda c, k, x: (0, lax.bitwise_xor(x[0], k) * N_C + c)
            ),
            scratch_shapes=[
                pltpu.VMEM((HEAD // CAP * tok, N_Z * HEAD), BF),
                pltpu.VMEM(((packed // CAP - HEAD // CAP) * tok, total - N_Z * HEAD), BF),
                pltpu.VMEM((tok, width // N_C), BF),
            ],
        ),
        out_shape=like(tok, width),
        compiler_params=params(SHARE),
        cost_estimate=cost(COST),
        name="combine_rows",
    )(x, tab, back.reshape(N_Z, N_C, packed, BLK))


def gather_x(piece, near):
    far_side = near ^ 2
    got = {near: swap(piece, "x", near), far_side: swap(piece, "x", far_side)}
    return [piece, got[1], swap(got[far_side], "x", near), got[3]]


def scatter_x(here, pair, other, near):
    moved = swap(pair, "x", near)
    joint = (other.astype(F32) + moved[1].astype(F32)).astype(BF)
    return here, moved, swap(joint, "x", near ^ 2)


def gather_y(rows, step):
    ahead, behind = shift(rows, "y", -1), shift(rows, "y", 1)
    far = shift(behind if step == 1 else ahead, "y", step)
    return [rows, ahead, far, behind]


def scatter_y(pieces):
    return [pieces[0]] + [shift(pieces[k], "y", k) for k in (2, 1, 3)]


ANY = pl.BlockSpec(memory_space=pl.ANY)


def stacked(rows):
    return jnp.concatenate([r[...] for r in rows], axis=0)


def fetch(weights, lo, hi, buf, sem):
    k = pl.program_id(0)

    @pl.when(k == 0)
    def _():
        for j, w in enumerate(weights):
            pltpu.make_async_copy(
                w.at[:, pl.ds(lo, hi - lo)], buf.at[j], sem.at[j]
            ).start()

    for s in range(2):
        j = 2 * k + s
        pltpu.make_async_copy(
            weights[0].at[:, pl.ds(lo, hi - lo)], buf.at[j], sem.at[j]
        ).wait()
    return jnp.concatenate([buf[2 * k], buf[2 * k + 1]], axis=1)


def fetch_scratch(weights, lo, hi):
    count = len(weights)
    return [
        pltpu.VMEM((count, weights[0].shape[0], hi - lo), BF),
        pltpu.SemaphoreType.DMA((count,)),
    ]


def row_specs(count, chunk, seg):
    return [pl.BlockSpec((chunk, seg), lambda k: (0, k))] * count


def whole(shape):
    return pl.BlockSpec(shape, lambda k: (0,) * len(shape))


def project_kernel(lo, hi, *refs):
    rows, weights, (out_ref, buf, sem) = refs[:N_Y], refs[N_Y:-3], refs[-3:]
    part = dot_nn(stacked(rows), fetch(weights, lo, hi, buf, sem))

    @pl.when(pl.program_id(0) == 0)
    def _():
        out_ref[...] = part

    @pl.when(pl.program_id(0) > 0)
    def _():
        out_ref[...] += part


def project(rows, weights, lo, hi):
    chunk = rows[0].shape[0]
    seg = weights[0].shape[0]
    shape = (chunk * N_Y, 2 * (hi - lo))
    return pl.pallas_call(
        functools.partial(project_kernel, lo, hi),
        grid=(N_X,),
        in_specs=row_specs(N_Y, chunk, seg) + [ANY] * len(weights),
        out_specs=whole(shape),
        out_shape=like(*shape, dtype=F32),
        scratch_shapes=fetch_scratch(weights, lo, hi),
        compiler_params=params(SHARE),
        cost_estimate=cost(COST),
        name="project_rows",
    )(*rows, *weights)


def sum_cores(half, other):
    mid = half.shape[1] // 2
    return half[...] + jnp.concatenate([other[:, mid:], other[:, :mid]], axis=1)


def gates(pre, hid):
    for s in range(2):
        gate = pre[:, 2 * s * hid : (2 * s + 1) * hid]
        yield gate, pre[:, (2 * s + 1) * hid : (2 * s + 2) * hid], jax.nn.sigmoid(gate)


def spread_back(value_ref, weights, outs):
    part = lax.dot_general(
        value_ref[...], weights, (((1,), (1,)), ((), ())), preferred_element_type=F32
    ).astype(BF)
    chunk = part.shape[0] // N_Y
    for i, ref in enumerate(outs):
        ref[...] = part[i * chunk : (i + 1) * chunk]


def forward_kernel(lo, hi, half_ref, other_ref, *refs):
    weights, hidden_ref, outs, (buf, sem) = refs[:-7], refs[-7], refs[-6:-2], refs[-2:]

    @pl.when(pl.program_id(0) == 0)
    def _():
        pre = sum_cores(half_ref, other_ref)
        parts = [gate * sig * up for gate, up, sig in gates(pre, pre.shape[1] // 4)]
        hidden_ref[...] = jnp.concatenate(parts, axis=1).astype(BF)

    spread_back(hidden_ref, fetch(weights, lo, hi, buf, sem), outs)


def backward_kernel(lo, hi, half_ref, other_ref, ghalf_ref, gother_ref, *refs):
    weights, grad_ref, outs, (buf, sem) = refs[:-7], refs[-7], refs[-6:-2], refs[-2:]

    @pl.when(pl.program_id(0) == 0)
    def _():
        pre = sum_cores(half_ref, other_ref)
        hid = pre.shape[1] // 4
        grad_hidden = sum_cores(ghalf_ref, gother_ref)
        parts = []
        for s, (gate, up, sig) in enumerate(gates(pre, hid)):
            grad = grad_hidden[:, s * hid : (s + 1) * hid]
            parts += [grad * up * sig * (1.0 + gate * (1.0 - sig)), grad * (gate * sig)]
        grad_ref[...] = jnp.concatenate(parts, axis=1).astype(BF)

    spread_back(grad_ref, fetch(weights, lo, hi, buf, sem), outs)


def middle(kernel, name, halves, weights, lo, hi):
    count = halves[0].shape[0]
    seg = weights[0].shape[0]
    chunk = count // N_Y
    cols = 2 * (hi - lo)
    first, *pieces = pl.pallas_call(
        functools.partial(kernel, lo, hi),
        grid=(N_X,),
        in_specs=[whole(h.shape) for h in halves] + [ANY] * len(weights),
        out_specs=[whole((count, cols))]
        + row_specs(N_Y, chunk, seg),
        out_shape=[like(count, cols)] + [like(chunk, N_X * seg)] * N_Y,
        scratch_shapes=fetch_scratch(weights, lo, hi),
        compiler_params=params(SHARE),
        cost_estimate=cost(COST),
        name=name,
    )(*halves, *weights)
    return first, pieces


def weight_grad_kernel(hidden_ref, grad_ref, *refs):
    tok, cot, outs = refs[:N_Y], refs[N_Y : 2 * N_Y], refs[2 * N_Y : -2]
    buf, sem = refs[-2:]
    k = pl.program_id(0)
    hid = hidden_ref.shape[1] // 2
    dims = (((0,), (0,)), ((), ()))
    gate_up = lax.dot_general(stacked(tok), grad_ref[...], dims, preferred_element_type=F32)
    down = lax.dot_general(stacked(cot), hidden_ref[...], dims, preferred_element_type=F32)
    for s in range(2):
        buf[2 * k + s, :, : 2 * hid] = gate_up[:, 2 * s * hid : (2 * s + 2) * hid].astype(BF)
        buf[2 * k + s, :, 2 * hid :] = down[:, s * hid : (s + 1) * hid].astype(BF)
    def copies(j):
        for i, near in enumerate((1, 3)):
            here, pair, other = outs[3 * i : 3 * i + 3]
            dst = {0: here, near: pair.at[0], 2: pair.at[1], near ^ 2: other}[j]
            yield pltpu.make_async_copy(buf.at[2 * j + i], dst, sem.at[2 * j + i])

    for j in range(N_X):

        @pl.when(k == j)
        def _(j=j):
            for c in copies(j):
                c.start()

    @pl.when(k == N_X - 1)
    def _():
        for j in range(N_X):
            for c in copies(j):
                c.wait()


def weight_grad(hidden, grad_pre, tok_rows, cot_rows):
    hid = hidden.shape[1] // 2
    chunk, width = tok_rows[0].shape
    seg = width // N_X
    one, two = like(seg, 3 * hid), like(2, seg, 3 * hid)
    outs = [one, two, one, one, two, one]
    return pl.pallas_call(
        weight_grad_kernel,
        grid=(N_X,),
        in_specs=[whole(hidden.shape), whole(grad_pre.shape)]
        + row_specs(2 * N_Y, chunk, seg),
        out_specs=[ANY] * len(outs),
        out_shape=outs,
        scratch_shapes=[
            pltpu.VMEM((2 * N_X, seg, 3 * hid), BF),
            pltpu.SemaphoreType.DMA((2 * N_X,)),
        ],
        compiler_params=params(SHARE),
        cost_estimate=cost(COST),
        name="weight_grad",
    )(hidden, grad_pre, *tok_rows, *cot_rows)


def split_kernel(c_ref, keep_in, give_in, keep_ref, give_ref):
    del c_ref
    keep_ref[...] = keep_in[0].astype(BF)
    give_ref[...] = give_in[0].astype(BF)


def split_master(c, master):
    _, quarter, cols = master.shape
    seg = quarter // N_C
    out = like(seg, cols)
    return pl.pallas_call(
        split_kernel,
        grid_spec=pltpu.PrefetchScalarGridSpec(
            num_scalar_prefetch=1,
            grid=(1,),
            in_specs=[
                pl.BlockSpec((1, seg, cols), lambda i, c: (0, c[0], 0)),
                pl.BlockSpec((1, seg, cols), lambda i, c: (0, 1 - c[0], 0)),
            ],
            out_specs=[pl.BlockSpec((seg, cols), lambda i, c: (0, 0))] * 2,
        ),
        out_shape=[out, out],
        compiler_params=params(ROOM),
        cost_estimate=cost(COST),
        name="split_master",
    )(c, master, master)


def update_kernel(c_ref, master_ref, sums_ref, other_ref, *refs):
    *parts, new_ref, out_ref, grad_ref = refs
    here = pl.program_id(0) == c_ref[0]

    @pl.when(here)
    def _():
        grad_ref[...] = sum(p[...].astype(F32) for p in parts).astype(BF).astype(F32)

    @pl.when(jnp.logical_not(here))
    def _():
        grad_ref[...] = other_ref[...].astype(F32)

    seg, cols = grad_ref.shape
    hid = cols // 3
    ones = jnp.ones((8, hid), F32)
    means = []
    for g in range(3):
        grad = grad_ref[:, g * hid : (g + 1) * hid]
        total = lax.dot_general(
            ones,
            grad * grad,
            (((1,), (1,)), ((), ())),
            precision=lax.Precision.HIGHEST,
            preferred_element_type=F32,
        )
        means.append(total[:1] / hid)
    sums = sums_ref[0] + jnp.concatenate(means, axis=0)
    out_ref[0] = sums
    scale = LEARN_RATE / (jnp.sqrt(sums) + EPSILON)
    tall = jnp.concatenate([scale, jnp.zeros((125, seg), F32)], axis=0).T
    for g in range(3):
        span = pl.ds(g * hid, hid)
        new_ref[:, span] = (master_ref[0, :, span] - grad_ref[:, span] * tall[:, g : g + 1]).astype(BF)


def update(c, master, sums, other, *parts):
    _, quarter, cols = master.shape
    seg = quarter // N_C
    piece = pl.BlockSpec((seg, cols), lambda h, c: (0, 0))
    first = pl.BlockSpec((pl.squeezed, seg, cols), lambda h, c: (0, 0, 0))
    rows = pl.BlockSpec((seg, cols), lambda h, c: (h, 0))
    lanes = pl.BlockSpec((1, 3, seg), lambda h, c: (0, 0, h))
    return pl.pallas_call(
        update_kernel,
        grid_spec=pltpu.PrefetchScalarGridSpec(
            num_scalar_prefetch=1,
            grid=(N_C,),
            in_specs=[pl.BlockSpec((1, seg, cols), lambda h, c: (0, h, 0)), lanes]
            + [piece, piece, first, piece],
            out_specs=[rows, lanes],
            scratch_shapes=[pltpu.VMEM((seg, cols), F32)],
        ),
        out_shape=[like(quarter, cols), like(*sums.shape, dtype=F32)],
        compiler_params=params(SHARE),
        cost_estimate=cost(COST),
        name="update_master",
    )(c, master, sums, other, *parts)


def copy_kernel(in_ref, out_ref):
    out_ref[0] = in_ref[...]


def placed(rows):
    count, cols = rows.shape
    return pl.pallas_call(
        copy_kernel,
        grid=(2,),
        in_specs=[pl.BlockSpec((count // 2, cols), lambda i: (i, 0))],
        out_specs=pl.BlockSpec((1, count // 2, cols), lambda i: (0, i, 0)),
        out_shape=like(1, count, cols),
        compiler_params=params(SHARE),
        cost_estimate=cost(COST),
        name="place_weights",
    )(rows)


def exchange(blocks):
    return lax.all_to_all(blocks, ("z", "c"), split_axis=0, concat_axis=0, tiled=True)


def local(tokens, cotangent, route_ids, router_weights, master, accumulator):
    hid = master.shape[2] // 3
    x = lax.axis_index("x").reshape(1)
    core = lax.axis_index("c").reshape(1)
    merge = lambda a: a.reshape((N_Z * N_C,) + a.shape[2:])

    route_ids, router_weights = route_ids.T, router_weights.T
    tok_send, out_tab, in_tab = select(x, route_ids, router_weights, tokens, False, True)
    tok_packed = exchange(merge(tok_send))
    (cot_send,) = select(x, route_ids, router_weights, after(cotangent, tok_send), True, False)
    cot_packed = exchange(merge(cot_send))

    own, give = split_master(core, after(master, cot_send))
    got = swap_core(give)
    own_weights = gather_x(own, 1)
    got_weights = gather_x(got, 3)
    weights = [w for pair in zip(own_weights, got_weights) for w in pair]

    tok_packed = after(tok_packed, cot_send, got)
    tok_rows = gather_y(unpack(tok_packed), 1)
    cot_packed = after(cot_packed, tok_rows[1], got_weights[1], got_weights[3])
    cot_rows = gather_y(unpack(cot_packed), -1)

    pre = project(tok_rows, weights, 0, 2 * hid)
    pre_other = swap_core(pre)
    hidden, out_pieces = middle(
        forward_kernel, "forward_rows", (pre, pre_other), weights, 2 * hid, 3 * hid
    )
    grad_hidden = project(cot_rows, weights, 2 * hid, 3 * hid)
    grad_other = after(swap_core(grad_hidden), hidden)
    grad_pre, in_pieces = middle(
        backward_kernel,
        "backward_rows",
        (pre, pre_other, grad_hidden, grad_other),
        weights,
        0,
        2 * hid,
    )
    grads = weight_grad(hidden, grad_pre, tok_rows, cot_rows)

    out_parts = scatter_y(out_pieces)
    in_pieces = [after(p, *grads[1::3]) for p in in_pieces]
    in_parts = scatter_y(in_pieces)
    own_parts = scatter_x(*grads[:3], 1)
    here, moved, joint = scatter_x(*grads[3:], 3)

    out_back = exchange(pack(*out_parts))
    in_back = exchange(pack(*in_parts))

    output = combine(x, out_tab, out_back)
    joint = after(joint, out_back)
    got_grad = sum(p.astype(F32) for p in (here, moved[0], joint)).astype(BF)
    new, sums = update(core, master, accumulator, swap_core(got_grad), *own_parts)
    new_weights = placed(swap_core(new))

    input_grad = combine(x, in_tab, in_back)
    return output, input_grad, new_weights, sums


def solution(mesh):
    fine = Mesh(mesh.devices.reshape(N_X, N_Z, N_Y, N_C), ("x", "z", "y", "c"))
    rows = P(("x", "z", "y", "c"), None)
    weights = P(("z", "y", "c"), "x", None)
    sums = P(("z", "y", "c"), None, "x")
    return jax.shard_map(
        local,
        mesh=fine,
        in_specs=(rows, rows, rows, rows, weights, sums),
        out_specs=(rows, rows, weights, sums),
        check_vma=False,
    )
```

```python
import functools

import jax
import jax.numpy as jnp
from jax import lax
from jax.experimental import pallas as pl
from jax.experimental.pallas import tpu as pltpu
from jax.sharding import Mesh, PartitionSpec as P


N_X, N_Z, N_Y, N_C = 4, 8, 4, 2
CAP = 5
LEARN_RATE = 0.01
EPSILON = 1e-06
BF = jnp.bfloat16
F32 = jnp.float32
COST = 100
ROOM = 60
SHARE = 28
BLK = 256


def swap_core(a):
    return lax.ppermute(a, "c", [(0, 1), (1, 0)])


def swap(a, axis, bits):
    return lax.ppermute(a, axis, [(i, i ^ bits) for i in range(lax.axis_size(axis))])


def shift(a, axis, step):
    n = lax.axis_size(axis)
    return lax.ppermute(a, axis, [(i, (i + step) % n) for i in range(n)])


def after(value, *firsts):
    return lax.optimization_barrier((value, *firsts))[0]


def iota(shape, dim):
    return lax.broadcasted_iota(jnp.int32, shape, dim)


def params(mib, **kw):
    return pltpu.CompilerParams(vmem_limit_bytes=mib << 20, **kw)


def like(*shape, dtype=BF):
    return jax.ShapeDtypeStruct(shape, dtype)


def dot_nn(a, b):
    return jnp.dot(a, b, preferred_element_type=F32)


def dot_nt(a, b):
    return lax.dot_general(a, b, (((1,), (1,)), ((), ())), preferred_element_type=F32)


def dot_tn(a, b):
    return lax.dot_general(a, b, (((0,), (0,)), ((), ())), preferred_element_type=F32)


def cost(micros):
    return pl.CostEstimate(
        flops=micros * 10**9, bytes_accessed=micros * 10**6, transcendentals=0
    )


HEAD = 8 * CAP


def table_lanes(packed):
    l = iota((1, N_Z * packed), 1)
    tail = packed - HEAD
    low = l < N_Z * HEAD
    rest = l - N_Z * HEAD
    return jnp.where(low, l // HEAD, rest // tail), jnp.where(low, l % HEAD, HEAD + rest % tail)


def select_kernel(scaled, with_tab, x_ref, ids_ref, w_ref, *refs):
    del x_ref
    segs, refs = refs[:N_X], refs[N_X:]
    send_ref, refs = refs[0], refs[1:]
    if with_tab:
        (out_tab, in_tab), refs = refs[:2], refs[2:]
    head_ref, tail_ref, head_row, tail_row = refs
    tok = ids_ref.shape[1]
    packed = send_ref.shape[2]
    blocks = packed // CAP

    @pl.when(pl.program_id(0) == 0)
    def _():
        expert = iota((128, tok), 0)
        named = jnp.zeros((128, tok), F32)
        weight_t = jnp.zeros((128, tok), F32)
        for k in range(ids_ref.shape[0]):
            hit = ids_ref[k : k + 1, :] == expert
            named = jnp.where(hit, 1.0, named)
            weight_t = jnp.where(hit, w_ref[k : k + 1, :], weight_t)
        earlier = jnp.where(iota((tok, tok), 0) < iota((tok, tok), 1), 1.0, 0.0).astype(BF)
        place = dot_nn(named.astype(BF), earlier)
        code_t = jnp.where(named > 0, place + 1.0, 0.0)
        for sel_ref, row_ref, count in (
            (head_ref, head_row, HEAD),
            (tail_ref, tail_row, packed - HEAD),
        ):
            r = iota((count, 1), 0)
            slot = (r % CAP + 1).astype(F32)
            columns = sel_ref.shape[1]
            diag = r // CAP == iota((1, columns), 1) // tok
            for e in range(N_Z):
                span = pl.ds(e * count, count)
                picked = jnp.broadcast_to(code_t[e : e + 1, :], (count, tok)) == slot
                ones = jnp.where(picked, 1.0, 0.0)
                wide = jnp.concatenate([ones] * (columns // tok), axis=1)
                sel_ref[span, :] = jnp.where(diag, wide, 0.0).astype(BF)
                if scaled:
                    part = jnp.where(
                        picked, jnp.broadcast_to(weight_t[e : e + 1, :], (count, tok)), 0.0
                    )
                    row_ref[span, :] = jnp.broadcast_to(
                        jnp.sum(part, axis=1, keepdims=True), (count, 128)
                    )
        if with_tab:
            total = N_Z * packed
            code, weight = code_t.T.astype(BF), weight_t.T.astype(BF)
            e, r = table_lanes(packed)
            spread = jnp.where(e == iota((128, 1), 0), 1.0, 0.0).astype(BF)
            slot = jnp.where(r < blocks * CAP, (r % CAP + 1).astype(F32), -1.0)
            valid = dot_nn(code, spread) == slot
            in_tab[...] = jnp.where(valid, 1.0, 0.0).astype(BF)
            out_tab[...] = jnp.where(valid, dot_nn(weight, spread), 0.0).astype(BF)

    wide = jnp.concatenate([s[...] for s in segs], axis=1)
    heads = HEAD // CAP
    for sel_ref, row_ref, first, last, span in (
        (head_ref, head_row, 0, heads, pl.ds(0, HEAD)),
        (tail_ref, tail_row, heads, blocks, pl.ds(HEAD, packed - HEAD)),
    ):
        stack = jnp.concatenate(
            [wide[:, q * BLK : (q + 1) * BLK] for q in range(first, last)], axis=0
        )
        rows = dot_nn(sel_ref[...], stack)
        if scaled:
            rows = rows * row_ref[:, :1]
        send_ref[:, 0, span, :] = rows.astype(BF).reshape(N_Z, -1, BLK)


def packed_rows(width):
    blocks = width // N_C // BLK
    return -(-blocks * CAP // 8) * 8


def select(x, ids, weights, data, scaled, with_tab):
    tok, width = data.shape
    seg = width // (N_X * N_C)
    packed = packed_rows(width)
    blocks = packed // CAP
    total = N_Z * packed
    seg_spec = lambda k: pl.BlockSpec(
        (tok, seg), lambda c, x: (0, lax.bitwise_xor(x[0], k) * N_C + c)
    )
    out_specs = [pl.BlockSpec((N_Z, 1, packed, BLK), lambda c, x: (0, c, 0, 0))]
    out_shape = [like(N_Z, N_C, packed, BLK)]
    if with_tab:
        out_specs += [pl.BlockSpec((tok, total), lambda c, x: (0, 0))] * 2
        out_shape += [like(tok, total)] * 2
    return pl.pallas_call(
        functools.partial(select_kernel, scaled, with_tab),
        grid_spec=pltpu.PrefetchScalarGridSpec(
            num_scalar_prefetch=1,
            grid=(N_C,),
            in_specs=[
                pl.BlockSpec(ids.shape, lambda c, x: (0, 0)),
                pl.BlockSpec(weights.shape, lambda c, x: (0, 0)),
            ]
            + [seg_spec(k) for k in range(N_X)],
            out_specs=out_specs,
            scratch_shapes=[
                pltpu.VMEM((N_Z * HEAD, HEAD // CAP * tok), BF),
                pltpu.VMEM((total - N_Z * HEAD, (blocks - HEAD // CAP) * tok), BF),
                pltpu.VMEM((N_Z * HEAD, 128), F32),
                pltpu.VMEM((total - N_Z * HEAD, 128), F32),
            ],
        ),
        out_shape=out_shape,
        compiler_params=params(ROOM),
        cost_estimate=cost(COST),
        name="select_cot" if scaled else "select_tok",
    )(x, ids, weights, *([data] * N_X))


GROWS = N_Z * CAP


def unpack_kernel(in_ref, out_ref):
    packed = in_ref.shape[1]
    heads = HEAD // CAP
    groups = ((0, heads, 0, HEAD), (heads, packed // CAP, HEAD, packed))
    for first, last, low, high in groups:
        count = high - low
        row, col = iota(((last - first) * GROWS, 1), 0), iota((1, N_Z * count), 1)
        place = row % GROWS
        want = place // CAP * count + row // GROWS * CAP + place % CAP
        perm = jnp.where(col == want, 1.0, 0.0).astype(BF)
        out = dot_nn(perm, in_ref[:, low:high, :].reshape(N_Z * count, BLK))
        for q in range(last - first):
            cols = pl.ds((first + q) * BLK, BLK)
            out_ref[:, cols] = out[q * GROWS : (q + 1) * GROWS].astype(BF)


def unpack(packed):
    srcs, rows, _ = packed.shape
    width = rows // CAP * BLK
    return pl.pallas_call(
        unpack_kernel,
        grid=(srcs // N_Z,),
        in_specs=[pl.BlockSpec((N_Z, rows, BLK), lambda h: (h, 0, 0))],
        out_specs=pl.BlockSpec((GROWS, width), lambda h: (h, 0)),
        out_shape=like(srcs * CAP, width),
        compiler_params=params(SHARE),
        cost_estimate=cost(COST),
        name="unpack_rows",
    )(packed)


def pack_kernel(*refs):
    *parts, send_ref = refs
    packed = send_ref.shape[1]
    blocks = packed // CAP
    total = sum(r[...].astype(F32) for r in parts)
    heads = HEAD // CAP
    groups = ((0, heads, 0, HEAD), (heads, blocks, HEAD, packed))
    for first, last, low, high in groups:
        count = high - low
        stack = jnp.concatenate(
            [total[:, q * BLK : (q + 1) * BLK] for q in range(first, last)], axis=0
        ).astype(BF)
        row, col = iota((N_Z * count, 1), 0), iota((1, (last - first) * GROWS), 1)
        r = row % count
        want = r // CAP * GROWS + row // count * CAP + r % CAP
        valid = r < (last - first) * CAP
        perm = jnp.where(col == jnp.where(valid, want, -1), 1.0, 0.0).astype(BF)
        send_ref[:, low:high, :] = dot_nn(perm, stack).astype(BF).reshape(N_Z, count, BLK)


def pack(*parts):
    rows, width = parts[0].shape
    packed = packed_rows(width * N_C)
    return pl.pallas_call(
        pack_kernel,
        grid=(rows // GROWS,),
        in_specs=[pl.BlockSpec((GROWS, width), lambda h: (h, 0))] * len(parts),
        out_specs=pl.BlockSpec((N_Z, packed, BLK), lambda h: (h, 0, 0)),
        out_shape=like(rows // CAP, packed, BLK),
        compiler_params=params(SHARE),
        cost_estimate=cost(COST),
        name="pack_rows",
    )(*parts)


def combine_kernel(x_ref, tab_ref, back_ref, out_ref, head_ref, tail_ref, acc_ref):
    del x_ref
    c, k = pl.program_id(0), pl.program_id(1)
    tok, total = tab_ref.shape
    packed = back_ref.shape[2]
    seg = out_ref.shape[1]
    heads = HEAD // CAP
    tails = packed // CAP - heads
    cut = N_Z * HEAD

    @pl.when((c == 0) & (k == 0))
    def _():
        block = table_lanes(packed)[1] // CAP
        for q in range(heads):
            here = jnp.where(block[:, :cut] == q, 1.0, 0.0).astype(BF)
            head_ref[pl.ds(q * tok, tok), :] = tab_ref[:, :cut] * here
        for q in range(tails):
            here = jnp.where(block[:, cut:] == heads + q, 1.0, 0.0).astype(BF)
            tail_ref[pl.ds(q * tok, tok), :] = tab_ref[:, cut:] * here

    @pl.when(k == 0)
    def _():
        back = back_ref[:, 0]
        for ref, first, count, rows in (
            (head_ref, 0, heads, back[:, :HEAD]),
            (tail_ref, heads, tails, back[:, HEAD:]),
        ):
            out = dot_nn(ref[...], rows.reshape(ref.shape[1], BLK)).astype(BF)
            for q in range(count):
                acc_ref[:, pl.ds((first + q) * BLK, BLK)] = out[q * tok : (q + 1) * tok]

    for j in range(N_X):

        @pl.when(k == j)
        def _(j=j):
            out_ref[...] = acc_ref[:, pl.ds(j * seg, seg)]


def combine(x, tab, back):
    tok, total = tab.shape
    _, packed, _ = back.shape
    width = packed // CAP * BLK * N_C
    seg = width // (N_X * N_C)
    return pl.pallas_call(
        combine_kernel,
        grid_spec=pltpu.PrefetchScalarGridSpec(
            num_scalar_prefetch=1,
            grid=(N_C, N_X),
            in_specs=[
                pl.BlockSpec((tok, total), lambda c, k, x: (0, 0)),
                pl.BlockSpec((N_Z, 1, packed, BLK), lambda c, k, x: (0, c, 0, 0)),
            ],
            out_specs=pl.BlockSpec(
                (tok, seg), lambda c, k, x: (0, lax.bitwise_xor(x[0], k) * N_C + c)
            ),
            scratch_shapes=[
                pltpu.VMEM((HEAD // CAP * tok, N_Z * HEAD), BF),
                pltpu.VMEM(((packed // CAP - HEAD // CAP) * tok, total - N_Z * HEAD), BF),
                pltpu.VMEM((tok, width // N_C), BF),
            ],
        ),
        out_shape=like(tok, width),
        compiler_params=params(SHARE),
        cost_estimate=cost(COST),
        name="combine_rows",
    )(x, tab, back.reshape(N_Z, N_C, packed, BLK))


def gather_x(piece, near):
    far_side = near ^ 2
    got = {near: swap(piece, "x", near), far_side: swap(piece, "x", far_side)}
    return [piece, got[1], swap(got[far_side], "x", near), got[3]]


def scatter_x(here, pair, other, near):
    moved = swap(pair, "x", near)
    joint = (other.astype(F32) + moved[1].astype(F32)).astype(BF)
    return here, moved, swap(joint, "x", near ^ 2)


def gather_y(rows, step):
    ahead, behind = shift(rows, "y", -1), shift(rows, "y", 1)
    far = shift(behind if step == 1 else ahead, "y", step)
    return [rows, ahead, far, behind]


def scatter_y(pieces):
    return [pieces[0]] + [shift(pieces[k], "y", k) for k in (2, 1, 3)]


ANY = pl.BlockSpec(memory_space=pl.ANY)


def stacked(rows):
    return jnp.concatenate([r[...] for r in rows], axis=0)


def fetch(weights, lo, hi, buf, sem):
    k = pl.program_id(0)

    @pl.when(k == 0)
    def _():
        for j, w in enumerate(weights):
            pltpu.make_async_copy(
                w.at[:, pl.ds(lo, hi - lo)], buf.at[j], sem.at[j]
            ).start()

    for s in range(2):
        j = 2 * k + s
        pltpu.make_async_copy(
            weights[0].at[:, pl.ds(lo, hi - lo)], buf.at[j], sem.at[j]
        ).wait()
    return jnp.concatenate([buf[2 * k], buf[2 * k + 1]], axis=1)


def fetch_scratch(weights, lo, hi):
    count = len(weights)
    return [
        pltpu.VMEM((count, weights[0].shape[0], hi - lo), BF),
        pltpu.SemaphoreType.DMA((count,)),
    ]


def row_specs(count, chunk, seg):
    return [pl.BlockSpec((chunk, seg), lambda k: (0, k))] * count


def whole(shape):
    return pl.BlockSpec(shape, lambda k: (0,) * len(shape))


def project_kernel(lo, hi, *refs):
    rows, weights, (out_ref, buf, sem) = refs[:N_Y], refs[N_Y:-3], refs[-3:]
    part = dot_nn(stacked(rows), fetch(weights, lo, hi, buf, sem))

    @pl.when(pl.program_id(0) == 0)
    def _():
        out_ref[...] = part

    @pl.when(pl.program_id(0) > 0)
    def _():
        out_ref[...] += part


def project(rows, weights, lo, hi):
    chunk = rows[0].shape[0]
    seg = weights[0].shape[0]
    shape = (chunk * N_Y, 2 * (hi - lo))
    return pl.pallas_call(
        functools.partial(project_kernel, lo, hi),
        grid=(N_X,),
        in_specs=row_specs(N_Y, chunk, seg) + [ANY] * len(weights),
        out_specs=whole(shape),
        out_shape=like(*shape, dtype=F32),
        scratch_shapes=fetch_scratch(weights, lo, hi),
        compiler_params=params(SHARE),
        cost_estimate=cost(COST),
        name="project_rows",
    )(*rows, *weights)


def sum_cores(half, other):
    mid = half.shape[1] // 2
    return half[...] + jnp.concatenate([other[:, mid:], other[:, :mid]], axis=1)


def gates(pre, hid):
    for s in range(2):
        gate = pre[:, 2 * s * hid : (2 * s + 1) * hid]
        yield gate, pre[:, (2 * s + 1) * hid : (2 * s + 2) * hid], jax.nn.sigmoid(gate)


def spread_back(value_ref, weights, outs):
    part = lax.dot_general(
        value_ref[...], weights, (((1,), (1,)), ((), ())), preferred_element_type=F32
    ).astype(BF)
    chunk = part.shape[0] // N_Y
    for i, ref in enumerate(outs):
        ref[...] = part[i * chunk : (i + 1) * chunk]


def forward_kernel(lo, hi, half_ref, other_ref, *refs):
    weights, hidden_ref, outs, (buf, sem) = refs[:-7], refs[-7], refs[-6:-2], refs[-2:]

    @pl.when(pl.program_id(0) == 0)
    def _():
        pre = sum_cores(half_ref, other_ref)
        parts = [gate * sig * up for gate, up, sig in gates(pre, pre.shape[1] // 4)]
        hidden_ref[...] = jnp.concatenate(parts, axis=1).astype(BF)

    spread_back(hidden_ref, fetch(weights, lo, hi, buf, sem), outs)


def backward_kernel(lo, hi, half_ref, other_ref, ghalf_ref, gother_ref, *refs):
    weights, grad_ref, outs, (buf, sem) = refs[:-7], refs[-7], refs[-6:-2], refs[-2:]

    @pl.when(pl.program_id(0) == 0)
    def _():
        pre = sum_cores(half_ref, other_ref)
        hid = pre.shape[1] // 4
        grad_hidden = sum_cores(ghalf_ref, gother_ref)
        parts = []
        for s, (gate, up, sig) in enumerate(gates(pre, hid)):
            grad = grad_hidden[:, s * hid : (s + 1) * hid]
            parts += [grad * up * sig * (1.0 + gate * (1.0 - sig)), grad * (gate * sig)]
        grad_ref[...] = jnp.concatenate(parts, axis=1).astype(BF)

    spread_back(grad_ref, fetch(weights, lo, hi, buf, sem), outs)


def middle(kernel, name, halves, weights, lo, hi):
    count = halves[0].shape[0]
    seg = weights[0].shape[0]
    chunk = count // N_Y
    cols = 2 * (hi - lo)
    first, *pieces = pl.pallas_call(
        functools.partial(kernel, lo, hi),
        grid=(N_X,),
        in_specs=[whole(h.shape) for h in halves] + [ANY] * len(weights),
        out_specs=[whole((count, cols))]
        + row_specs(N_Y, chunk, seg),
        out_shape=[like(count, cols)] + [like(chunk, N_X * seg)] * N_Y,
        scratch_shapes=fetch_scratch(weights, lo, hi),
        compiler_params=params(SHARE),
        cost_estimate=cost(COST),
        name=name,
    )(*halves, *weights)
    return first, pieces


def weight_grad_kernel(hidden_ref, grad_ref, *refs):
    tok, cot, outs = refs[:N_Y], refs[N_Y : 2 * N_Y], refs[2 * N_Y : -2]
    buf, sem = refs[-2:]
    k = pl.program_id(0)
    hid = hidden_ref.shape[1] // 2
    dims = (((0,), (0,)), ((), ()))
    gate_up = lax.dot_general(stacked(tok), grad_ref[...], dims, preferred_element_type=F32)
    down = lax.dot_general(stacked(cot), hidden_ref[...], dims, preferred_element_type=F32)
    for s in range(2):
        buf[2 * k + s, :, : 2 * hid] = gate_up[:, 2 * s * hid : (2 * s + 2) * hid].astype(BF)
        buf[2 * k + s, :, 2 * hid :] = down[:, s * hid : (s + 1) * hid].astype(BF)
    def copies(j):
        for i, near in enumerate((1, 3)):
            here, pair, other = outs[3 * i : 3 * i + 3]
            dst = {0: here, near: pair.at[0], 2: pair.at[1], near ^ 2: other}[j]
            yield pltpu.make_async_copy(buf.at[2 * j + i], dst, sem.at[2 * j + i])

    for j in range(N_X):

        @pl.when(k == j)
        def _(j=j):
            for c in copies(j):
                c.start()

    @pl.when(k == N_X - 1)
    def _():
        for j in range(N_X):
            for c in copies(j):
                c.wait()


def weight_grad(hidden, grad_pre, tok_rows, cot_rows):
    hid = hidden.shape[1] // 2
    chunk, width = tok_rows[0].shape
    seg = width // N_X
    one, two = like(seg, 3 * hid), like(2, seg, 3 * hid)
    outs = [one, two, one, one, two, one]
    return pl.pallas_call(
        weight_grad_kernel,
        grid=(N_X,),
        in_specs=[whole(hidden.shape), whole(grad_pre.shape)]
        + row_specs(2 * N_Y, chunk, seg),
        out_specs=[ANY] * len(outs),
        out_shape=outs,
        scratch_shapes=[
            pltpu.VMEM((2 * N_X, seg, 3 * hid), BF),
            pltpu.SemaphoreType.DMA((2 * N_X,)),
        ],
        compiler_params=params(SHARE),
        cost_estimate=cost(COST),
        name="weight_grad",
    )(hidden, grad_pre, *tok_rows, *cot_rows)


def split_kernel(c_ref, keep_in, give_in, keep_ref, give_ref):
    del c_ref
    keep_ref[...] = keep_in[0].astype(BF)
    give_ref[...] = give_in[0].astype(BF)


def split_master(c, master):
    _, quarter, cols = master.shape
    seg = quarter // N_C
    out = like(seg, cols)
    return pl.pallas_call(
        split_kernel,
        grid_spec=pltpu.PrefetchScalarGridSpec(
            num_scalar_prefetch=1,
            grid=(1,),
            in_specs=[
                pl.BlockSpec((1, seg, cols), lambda i, c: (0, c[0], 0)),
                pl.BlockSpec((1, seg, cols), lambda i, c: (0, 1 - c[0], 0)),
            ],
            out_specs=[pl.BlockSpec((seg, cols), lambda i, c: (0, 0))] * 2,
        ),
        out_shape=[out, out],
        compiler_params=params(ROOM),
        cost_estimate=cost(COST),
        name="split_master",
    )(c, master, master)


def update_kernel(c_ref, master_ref, sums_ref, other_ref, *refs):
    *parts, new_ref, out_ref, grad_ref = refs
    here = pl.program_id(0) == c_ref[0]

    @pl.when(here)
    def _():
        grad_ref[...] = sum(p[...].astype(F32) for p in parts).astype(BF).astype(F32)

    @pl.when(jnp.logical_not(here))
    def _():
        grad_ref[...] = other_ref[...].astype(F32)

    seg, cols = grad_ref.shape
    hid = cols // 3
    ones = jnp.ones((8, hid), F32)
    means = []
    for g in range(3):
        grad = grad_ref[:, g * hid : (g + 1) * hid]
        total = lax.dot_general(
            ones,
            grad * grad,
            (((1,), (1,)), ((), ())),
            precision=lax.Precision.HIGHEST,
            preferred_element_type=F32,
        )
        means.append(total[:1] / hid)
    sums = sums_ref[0] + jnp.concatenate(means, axis=0)
    out_ref[0] = sums
    scale = LEARN_RATE / (jnp.sqrt(sums) + EPSILON)
    tall = jnp.concatenate([scale, jnp.zeros((125, seg), F32)], axis=0).T
    for g in range(3):
        span = pl.ds(g * hid, hid)
        new_ref[:, span] = (master_ref[0, :, span] - grad_ref[:, span] * tall[:, g : g + 1]).astype(BF)


def update(c, master, sums, other, *parts):
    _, quarter, cols = master.shape
    seg = quarter // N_C
    piece = pl.BlockSpec((seg, cols), lambda h, c: (0, 0))
    first = pl.BlockSpec((pl.squeezed, seg, cols), lambda h, c: (0, 0, 0))
    rows = pl.BlockSpec((seg, cols), lambda h, c: (h, 0))
    lanes = pl.BlockSpec((1, 3, seg), lambda h, c: (0, 0, h))
    return pl.pallas_call(
        update_kernel,
        grid_spec=pltpu.PrefetchScalarGridSpec(
            num_scalar_prefetch=1,
            grid=(N_C,),
            in_specs=[pl.BlockSpec((1, seg, cols), lambda h, c: (0, h, 0)), lanes]
            + [piece, piece, first, piece],
            out_specs=[rows, lanes],
            scratch_shapes=[pltpu.VMEM((seg, cols), F32)],
        ),
        out_shape=[like(quarter, cols), like(*sums.shape, dtype=F32)],
        compiler_params=params(SHARE),
        cost_estimate=cost(COST),
        name="update_master",
    )(c, master, sums, other, *parts)


def copy_kernel(in_ref, out_ref):
    out_ref[0] = in_ref[...]


def placed(rows):
    count, cols = rows.shape
    return pl.pallas_call(
        copy_kernel,
        grid=(2,),
        in_specs=[pl.BlockSpec((count // 2, cols), lambda i: (i, 0))],
        out_specs=pl.BlockSpec((1, count // 2, cols), lambda i: (0, i, 0)),
        out_shape=like(1, count, cols),
        compiler_params=params(SHARE),
        cost_estimate=cost(COST),
        name="place_weights",
    )(rows)


def exchange(blocks):
    return lax.all_to_all(blocks, ("z", "c"), split_axis=0, concat_axis=0, tiled=True)


def local(tokens, cotangent, route_ids, router_weights, master, accumulator):
    hid = master.shape[2] // 3
    x = lax.axis_index("x").reshape(1)
    core = lax.axis_index("c").reshape(1)
    merge = lambda a: a.reshape((N_Z * N_C,) + a.shape[2:])

    route_ids, router_weights = route_ids.T, router_weights.T
    tok_send, out_tab, in_tab = select(x, route_ids, router_weights, tokens, False, True)
    tok_packed = exchange(merge(tok_send))
    (cot_send,) = select(x, route_ids, router_weights, after(cotangent, tok_send), True, False)
    cot_packed = exchange(merge(cot_send))

    own, give = split_master(core, after(master, cot_send))
    got = swap_core(give)
    own_weights = gather_x(own, 1)
    got_weights = gather_x(got, 3)
    weights = [w for pair in zip(own_weights, got_weights) for w in pair]

    tok_packed = after(tok_packed, cot_send, got)
    tok_rows = gather_y(unpack(tok_packed), 1)
    cot_packed = after(cot_packed, tok_rows[1], got_weights[1], got_weights[3])
    cot_rows = gather_y(unpack(cot_packed), -1)

    pre = project(tok_rows, weights, 0, 2 * hid)
    pre_other = swap_core(pre)
    hidden, out_pieces = middle(
        forward_kernel, "forward_rows", (pre, pre_other), weights, 2 * hid, 3 * hid
    )
    grad_hidden = project(cot_rows, weights, 2 * hid, 3 * hid)
    grad_other = after(swap_core(grad_hidden), hidden)
    grad_pre, in_pieces = middle(
        backward_kernel,
        "backward_rows",
        (pre, pre_other, grad_hidden, grad_other),
        weights,
        0,
        2 * hid,
    )
    grads = weight_grad(hidden, grad_pre, tok_rows, cot_rows)

    out_parts = scatter_y(out_pieces)
    in_pieces = [after(p, *grads[1::3]) for p in in_pieces]
    in_parts = scatter_y(in_pieces)
    own_parts = scatter_x(*grads[:3], 1)
    here, moved, joint = scatter_x(*grads[3:], 3)

    out_back = exchange(pack(*out_parts))
    in_back = exchange(pack(*in_parts))

    output = combine(x, out_tab, out_back)
    joint = after(joint, out_back)
    got_grad = sum(p.astype(F32) for p in (here, moved[0], joint)).astype(BF)
    new, sums = update(core, master, accumulator, swap_core(got_grad), *own_parts)
    new_weights = placed(swap_core(new))

    input_grad = combine(x, in_tab, in_back)
    return output, input_grad, new_weights, sums


def solution(mesh):
    fine = Mesh(mesh.devices.reshape(N_X, N_Z, N_Y, N_C), ("x", "z", "y", "c"))
    rows = P(("x", "z", "y", "c"), None)
    weights = P(("z", "y", "c"), "x", None)
    sums = P(("z", "y", "c"), None, "x")
    return jax.shard_map(
        local,
        mesh=fine,
        in_specs=(rows, rows, rows, rows, weights, sums),
        out_specs=(rows, rows, weights, sums),
        check_vma=False,
    )
```
